32 devices in a mesh: row: 4 (over y, x), col: 4 (over z), panel: 2 (over core).
Axes of the slice: x: 2, y: 2, z: 4, core: 2. Of those that a mesh axis runs over, the one named last changes fastest.
Arguments:
- basis_values: bfloat16 [512, 2048, 128], P(('row', 'col', 'panel')), may hold values from -6 to 6
- potential: float32 [65536], P(('row', 'col', 'panel')), may hold values from -0.0014648438 to 0.0014648438
- pair_atoms: int32 [2, 4096], P(None, ('row', 'col', 'panel')), may hold values from 0 to 15
- target_device: int32 [4096, 1], P(('row', 'col', 'panel')), may hold values from 0 to 31; in each aligned block of 128 rows (0 to 127, 128 to 255, ...) at most 6 rows name the same one
- target_block: int32 [4096], P(('row', 'col', 'panel')), may hold values from 0 to 1
- density: bfloat16 [1024, 1024], P('row', 'col'), may hold values from -0.3125 to 0.3125
- density_mask: int32 [8, 8], P('row', 'col'), may hold values 0 or 1
- inverse_intersection: bfloat16 [1024, 2048], P('row', 'col'), may hold values from -6 to 6
- inverse_mask: int32 [8, 16], P('row', 'col'), may hold values 0 or 1
Outputs:
- gradient: float32 [1024, 2048], P('row', ('col', 'panel'))
The draws below stay inside these ranges and needn't reach their ends.
Inputs may be any that keep to these rules, and one draw needn't show every extreme that they name: `target_device`: among the 128 rows of one device no owner appears more than 6 times.
All inputs are finite; a program needn't handle non-finite values. No bound on the sum of `density_mask` or of `inverse_mask` on one device may be relied on, other than what follows from the above.
Results may differ from the reference program's by a relative error of at most 0.0058.
Values may be sent and summed in bfloat16 or wider, within the bound.
No kernel may reach another device: no remote copies, remote signals or barrier semaphores. Data moves between devices by JAX's collectives and lax.ppermute only.
A program may use at most 128 MiB of HBM per device.

```python
import math
import jax
import jax.numpy as jnp
import numpy as np
from jax import lax

BS = 128
TB = 2
GP = 2048
NA = 16
PART_DEV = 128
NB = 8
PW = 2048
PARTS_SIZE = 4096
CAP = 6
N_ROW = 4
N_COL = 4
N_PANEL = 2
DEVICES = 32


def set_ends(values, stream_key, low, largest):
    dims = values.shape
    place = [jax.random.randint(jax.random.fold_in(stream_key, axis), (), 0, dims[axis]) for axis in range(len(dims))]
    values = values.at[tuple(place)].set(low)
    longest = dims.index(max(dims))
    place[longest] = (place[longest] + 1) % dims[longest]
    return values.at[tuple(place)].set(largest)


def level_of(own_key, shape, cuts, smallest, high):
    level = 1.0
    for dim, blocks in cuts:
        steps = jax.random.uniform(jax.random.fold_in(jax.random.fold_in(own_key, 6), dim), (blocks,), jnp.float32, smallest / len(cuts), high / len(cuts))
        level = level * jnp.repeat(jnp.exp(steps), shape[dim] // blocks).reshape((-1,) + (1,) * (len(shape) - 1 - dim))
    return level


def assign_block(rng, own, number, rows, count, top, limit, skew):
    ranking = jax.random.permutation(rng, count)
    crowded, usual = load_shares(count, rows * top, limit, skew, True), load_shares(count, rows * top, limit, skew, False)
    places = jnp.arange(count)

    def named(sizes, turn):
        used = int((sizes > 0).sum())
        fixed = max(1, used // 4)
        shifted = fixed + (places - fixed + turn * (used - fixed)) % max(1, count - fixed)
        return jnp.zeros((count,), jnp.int32).at[ranking[jnp.where(places < fixed, places, shifted)]].set(jnp.asarray(sizes, jnp.int32))

    sizes = jnp.where(number % 4 == 0, named(crowded, number // 4), named(usual, number - number // 4 - 1))
    mixed = jax.random.permutation(jax.random.fold_in(own, 3), count)
    giver, sink = mixed[0:count // 2 * 2:2], mixed[1:count // 2 * 2:2]
    slack = jnp.minimum(sizes[giver] - 1, limit - sizes[sink]) // 2
    slack = jnp.where((giver == ranking[0]) | (sink == ranking[0]) | (sizes[sink] == 0), 0, jnp.maximum(slack, 0))
    shifted = jax.random.randint(jax.random.fold_in(own, 4), (count // 2,), 0, 1 << 20) % (slack + 1)
    sizes = sizes.at[giver].add(-shifted).at[sink].add(shifted)
    members = jnp.searchsorted(jnp.cumsum(sizes), jnp.arange(rows * top), side="right").astype(jnp.int32)
    listing = members.reshape(top, rows).T
    listing = listing[jax.random.permutation(jax.random.fold_in(own, 1), rows)]
    turn = jax.random.randint(jax.random.fold_in(own, 2), (rows, 1), 0, top)
    return jnp.take_along_axis(listing, (jnp.arange(top)[None, :] + turn) % top, axis=1)


def load_shares(count, total, limit, lean, full):
    loads = [(1 << 20) // math.isqrt(grade ** lean) + 1 for grade in range(1, count + 1)]
    largest = limit if full else min(limit, max(-(-total // count), total * loads[0] // sum(loads)))
    least = 1 if total - largest >= count - 1 else 0
    counts, rest = [largest] + [least] * (count - 1), total - largest - least * (count - 1)
    while rest > 0:
        free = [i for i in range(1, count) if counts[i] < largest] or [i for i in range(1, count) if counts[i] < limit]
        mass, left = sum([loads[i] for i in free]), rest
        for i in free:
            more = min(limit - counts[i], max(1, left * loads[i] // mass), rest)
            counts[i] = counts[i] + more
            rest = rest - more
    return np.array(counts)


def gaussian(own_key, shape, scale, reach, split=(), kind=jnp.bfloat16):
    level = level_of(own_key, shape, split, -0.22, 0.18) if split else 1.0
    drawn = jax.random.normal(own_key, shape, jnp.float32) * scale * level
    return jnp.minimum(jnp.maximum(drawn, -reach), reach).astype(kind)


def setup_inputs(seed: int = 0) -> dict:
    streams_of = jax.random.split(jax.random.key(seed), 10)
    basis_values = gaussian(streams_of[0], (NA * DEVICES, GP, BS), 1.0, 6.0, ((0, 32),))
    potential = gaussian(streams_of[1], (GP * DEVICES,), (GP * NB * BS * 8) ** -0.5, 0.0014648438, ((0, 32),), jnp.float32)
    pair_atoms = set_ends(jax.random.randint(streams_of[2], (2, PARTS_SIZE), 0, NA), jax.random.fold_in(streams_of[2], 1), 0, NA - 1).astype(jnp.int32)
    target_device_keys = jax.random.split(jax.random.fold_in(streams_of[3], 1), PARTS_SIZE // PART_DEV)
    target_device_turns = jax.random.permutation(jax.random.fold_in(streams_of[3], 3), PARTS_SIZE // PART_DEV)
    target_device = jax.vmap(lambda own, number: assign_block(jax.random.fold_in(streams_of[3], 2), own, number, PART_DEV, DEVICES, 1, CAP, 2))(target_device_keys, target_device_turns).reshape((PARTS_SIZE, 1))
    target_block = set_ends(jax.random.randint(streams_of[4], (PARTS_SIZE,), 0, TB * TB // N_PANEL), jax.random.fold_in(streams_of[4], 1), 0, (TB * TB // N_PANEL) - 1).astype(jnp.int32)
    density = gaussian(streams_of[5], (NB * BS, NB * BS), (NB * BS // 3) ** -0.5, 0.3125, ((0, 4), (1, 4)))
    density_mask = set_ends((jax.random.randint(streams_of[6], (NB, NB), 0, 3) < 1).astype(jnp.int32), jax.random.fold_in(streams_of[6], 1), 0, 1)
    inverse_intersection = gaussian(streams_of[7], (NB * BS, PW), 1.0, 6.0, ((0, 4), (1, 4)))
    inverse_mask = set_ends((jax.random.randint(streams_of[8], (NB, PW // BS), 0, 2) < 1).astype(jnp.int32), jax.random.fold_in(streams_of[8], 1), 0, 1)
    return {"basis_values": basis_values, "potential": potential, "pair_atoms": pair_atoms, "target_device": target_device, "target_block": target_block, "density": density, "density_mask": density_mask, "inverse_intersection": inverse_intersection, "inverse_mask": inverse_mask}


def masked_blocks(matrix, block_mask):
    mask_rows, mask_cols = block_mask.shape
    shaped = matrix.reshape(mask_rows, BS, mask_cols, BS)
    factor = block_mask.astype(matrix.dtype)[:, None, :, None]
    return (shaped * factor).reshape(mask_rows * BS, mask_cols * BS)


def reference(basis_values, potential, pair_atoms, target_device, target_block, density, density_mask, inverse_intersection, inverse_mask):
    regions = N_ROW * N_COL * N_PANEL
    half_rows = TB // N_PANEL
    basis = basis_values.reshape(regions, NA, GP, BS)
    weights = potential.reshape(regions, GP)
    left_ids = pair_atoms[0].reshape(regions, PART_DEV)
    right_ids = pair_atoms[1].reshape(regions, PART_DEV)
    owner = target_device[:, 0]
    owner_row = owner // (N_COL * N_PANEL)
    owner_col = (owner // N_PANEL) % N_COL
    owner_layer = owner % N_PANEL
    block_row = owner_row * TB + owner_layer * half_rows + target_block // TB
    block_col = owner_col * TB + target_block % TB
    block_ids = (block_row * NB + block_col).astype(jnp.int32).reshape(regions, PART_DEV)

    def integrate(summed, inputs):
        region_basis, region_weights, left_pick, right_pick, region_blocks = inputs
        weighted = (region_basis.astype(jnp.float32) * region_weights[None, :, None]).astype(jnp.bfloat16)
        left_rows = region_basis[left_pick].astype(jnp.float32)
        right_rows = weighted[right_pick].astype(jnp.float32)
        partials = jnp.einsum("pgi,pgj->pij", left_rows, right_rows).astype(jnp.bfloat16)
        return summed.at[region_blocks].add(partials.astype(jnp.float32)), None

    summed = jnp.zeros((NB * NB, BS, BS), jnp.float32)
    summed, unused = lax.scan(integrate, summed, (basis, weights, left_ids, right_ids, block_ids))
    hamiltonian = summed.reshape(NB, NB, BS, BS).transpose(0, 2, 1, 3).reshape(NB * BS, NB * BS).astype(jnp.bfloat16)
    density_used = masked_blocks(density, density_mask)
    inverse_used = masked_blocks(inverse_intersection, inverse_mask)
    panel_product = jnp.dot(density_used, inverse_used, preferred_element_type=jnp.float32).astype(jnp.bfloat16)
    return jnp.dot(hamiltonian, panel_product, preferred_element_type=jnp.float32)
```

```python
import functools

import jax
import jax.numpy as jnp
from jax import lax
from jax.experimental import pallas as pl
from jax.experimental.pallas import tpu as pltpu
from jax.sharding import PartitionSpec as P

UNROLL = 4
VMEM_LIMIT = 60 * 1024 * 1024


def target(i, s, n):
    return i ^ s if n & (n - 1) == 0 else (i + s) % n


def source(i, s, n):
    return i ^ s if n & (n - 1) == 0 else (i - s) % n


def target_slot(i, j, n):
    return i ^ j if n & (n - 1) == 0 else (j - i) % n


def source_slot(i, j, n):
    return i ^ j if n & (n - 1) == 0 else (i - j) % n


def exchange(value, axis, slot):
    n = lax.axis_size(axis)
    return lax.ppermute(value, axis, [(i, target(i, slot, n)) for i in range(n)])


def masked_blocks(matrix, block_mask, block_size):
    mask_rows, mask_cols = block_mask.shape
    shaped = matrix.reshape(mask_rows, block_size, mask_cols, block_size)
    factor = block_mask.astype(matrix.dtype)[:, None, :, None]
    return (shaped * factor).reshape(mask_rows * block_size, mask_cols * block_size)


def integrate_body(
    blocks, left_ref, right_ref, slot_ref, basis_ref, pot_ref, keep_ref, send_ref,
    basis, weighted, pot_cols, total, sems, pending, unit_left, unit_rights, unit_slots,
):
    atoms, points, size = basis.shape
    parts = left_ref.shape[0]

    def fetch(a):
        return pltpu.make_async_copy(basis_ref.at[a], basis.at[a], sems.at[a])

    for a in range(atoms):
        fetch(a).start()

    for a in range(atoms):
        pending[a] = -1

    def plan(n, count):
        a = left_ref[n]
        earlier = pending[a]
        fresh = earlier < 0
        pending[a] = jnp.where(fresh, n, -1)

        @pl.when(jnp.logical_not(fresh))
        def _():
            unit_left[count] = a
            unit_rights[2 * count] = right_ref[earlier]
            unit_rights[2 * count + 1] = right_ref[n]
            unit_slots[2 * count] = slot_ref[earlier]
            unit_slots[2 * count + 1] = slot_ref[n]

        return count + jnp.where(fresh, 0, 1)

    def plan_single(a, count):
        earlier = pending[a]

        @pl.when(earlier >= 0)
        def _():
            unit_left[count] = a
            unit_rights[2 * count] = right_ref[earlier]
            unit_rights[2 * count + 1] = right_ref[earlier]
            unit_slots[2 * count] = slot_ref[earlier]
            unit_slots[2 * count + 1] = blocks

        return count + jnp.where(earlier >= 0, 1, 0)

    count = lax.fori_loop(0, parts, plan, 0)
    count = lax.fori_loop(0, atoms, plan_single, count)
    for i in range(UNROLL - 1):
        unit_left[count + i] = 0
        for j in range(2):
            unit_rights[2 * (count + i) + j] = 0
            unit_slots[2 * (count + i) + j] = blocks

    for k in range(points // size):
        row = pot_ref[k : k + 1, :]
        pot_cols[k * size : (k + 1) * size, :] = jnp.broadcast_to(row, (size, size)).T

    def clear(i, carry):
        total[i] = jnp.zeros((size, size), jnp.float32)
        return carry

    lax.fori_loop(0, blocks + 1, clear, 0)

    def weigh(a, carry):
        fetch(a).wait()
        for k in range(points // size):
            at = slice(k * size, (k + 1) * size)
            weighted[a, at, :] = (basis[a, at, :].astype(jnp.float32) * pot_cols[at, :]).astype(jnp.bfloat16)
        return carry

    lax.fori_loop(0, atoms, weigh, 0)

    def step(i, carry):
        for j in range(UNROLL):
            u = i * UNROLL + j
            rights = jnp.concatenate([weighted[unit_rights[2 * u]], weighted[unit_rights[2 * u + 1]]], axis=1)
            found = lax.dot_general(
                basis[unit_left[u]], rights, (((0,), (0,)), ((), ())), preferred_element_type=jnp.float32
            )
            total[unit_slots[2 * u]] += found[:, :size]
            total[unit_slots[2 * u + 1]] += found[:, size:]
        return carry

    lax.fori_loop(0, (count + UNROLL - 1) // UNROLL, step, 0)
    half = blocks // 2

    def put(i, carry):
        keep_ref[i] = total[i].astype(jnp.bfloat16)
        send_ref[i] = total[half + i].astype(jnp.bfloat16)
        return carry

    lax.fori_loop(0, half, put, 0)


def integrate(basis_values, potential, left, right, slots, blocks):
    atoms, points, size = basis_values.shape
    parts = left.shape[0]
    most = (parts + atoms) // 2 + UNROLL + 1
    smem = pl.BlockSpec(memory_space=pltpu.SMEM)
    vmem = pl.BlockSpec(memory_space=pltpu.VMEM)
    half = jax.ShapeDtypeStruct((blocks // 2, size, size), jnp.bfloat16)
    return pl.pallas_call(
        functools.partial(integrate_body, blocks),
        out_shape=(half, half),
        in_specs=[smem, smem, smem, pl.BlockSpec(memory_space=pl.ANY), vmem],
        out_specs=(vmem, vmem),
        scratch_shapes=[
            pltpu.VMEM((atoms, points, size), jnp.bfloat16),
            pltpu.VMEM((atoms, points, size), jnp.bfloat16),
            pltpu.VMEM((points, size), jnp.float32),
            pltpu.VMEM((blocks + 1, size, size), jnp.float32),
            pltpu.SemaphoreType.DMA((atoms,)),
            pltpu.SMEM((atoms,), jnp.int32),
            pltpu.SMEM((most,), jnp.int32),
            pltpu.SMEM((2 * most,), jnp.int32),
            pltpu.SMEM((2 * most,), jnp.int32),
        ],
        compiler_params=pltpu.CompilerParams(vmem_limit_bytes=VMEM_LIMIT),
        cost_estimate=pl.CostEstimate(
            flops=2 * parts * points * size * size,
            bytes_accessed=2 * basis_values.size + 2 * blocks * size * size,
            transcendentals=0,
        ),
        name="integrate",
    )(left, right, slots, basis_values, potential.reshape(points // size, size))


def product_body(count, index_ref, *refs):
    lefts, rights, out = refs[:count], refs[count : 2 * count], refs[-2]
    stacked = refs[-1]
    for s in range(count):
        stacked[s] = rights[s][...]
    found = jnp.dot(lefts[0][...], stacked[index_ref[0]], preferred_element_type=jnp.float32)
    for s in range(1, count):
        found += jnp.dot(lefts[s][...], stacked[index_ref[s]], preferred_element_type=jnp.float32)
    out[...] = found.astype(out.dtype)


def product(lefts, rights, index, dtype):
    count = len(lefts)
    rows, columns = lefts[0].shape[0], rights[0].shape[1]
    vmem = pl.BlockSpec(memory_space=pltpu.VMEM)
    return pl.pallas_call(
        functools.partial(product_body, count),
        out_shape=jax.ShapeDtypeStruct((rows, columns), dtype),
        in_specs=[pl.BlockSpec(memory_space=pltpu.SMEM)] + [vmem] * (2 * count),
        out_specs=vmem,
        scratch_shapes=[pltpu.VMEM((count,) + rights[0].shape, rights[0].dtype)],
        cost_estimate=pl.CostEstimate(
            flops=2 * count * rows * columns * rights[0].shape[0],
            bytes_accessed=2 * count * (lefts[0].size + rights[0].size),
            transcendentals=0,
        ),
        name="product",
    )(index, *lefts, *rights)


def gradient_body(count, index_ref, side_ref, own_ref, other_ref, *refs):
    rights, out, stacked = refs[:count], refs[-2], refs[-1]
    for s in range(count):
        stacked[s] = rights[s][...]
    blocks, size = own_ref.shape[1], own_ref.shape[2]
    side = side_ref[0]
    for which, ref in ((side, own_ref), (1 - side, other_ref)):
        found = None
        for s in range(count):
            left = jnp.concatenate([ref[s, b] for b in range(blocks)], axis=1)
            term = jnp.dot(left, stacked[index_ref[s]], preferred_element_type=jnp.float32)
            found = term if found is None else found + term
        out[pl.ds(which * size, size), :] = found


def local(
    basis_values,
    potential,
    pair_atoms,
    target_device,
    target_block,
    density,
    density_mask,
    inverse_intersection,
    inverse_mask,
):
    size = basis_values.shape[2]
    rows, cols, layers = lax.axis_size("row"), lax.axis_size("col"), lax.axis_size("panel")
    row, col, layer = lax.axis_index("row"), lax.axis_index("col"), lax.axis_index("panel")
    tile_blocks = density_mask.shape[0]
    per_owner = tile_blocks // layers * tile_blocks
    blocks = layers * rows * cols * per_owner

    width = inverse_intersection.shape[1] // layers
    mask_width = inverse_mask.shape[1] // layers
    density_used = masked_blocks(density, density_mask, size)
    inverse_used = masked_blocks(
        lax.dynamic_slice_in_dim(inverse_intersection, layer * width, width, 1),
        lax.dynamic_slice_in_dim(inverse_mask, layer * mask_width, mask_width, 1),
        size,
    )
    lefts = [density_used] + [exchange(density_used, "col", s) for s in range(1, cols)]
    rights = [inverse_used] + [exchange(inverse_used, "row", s) for s in range(1, rows)]

    owner = target_device[:, 0]
    there_row, there_col, there_layer = owner // (cols * layers), (owner // layers) % cols, owner % layers
    slots = target_slot(layer, there_layer, layers) * rows + target_slot(row, there_row, rows)
    slots = (slots * cols + target_slot(col, there_col, cols)) * per_owner + target_block
    keep, send = integrate(basis_values, potential, pair_atoms[0], pair_atoms[1], slots, blocks)

    index = jnp.stack([source_slot(row, source(col, s, cols), rows) for s in range(cols)])
    panel_tile = product(lefts, rights, index, jnp.bfloat16)
    panels = [panel_tile] + [exchange(panel_tile, "row", s) for s in range(1, rows)]

    def added(*terms):
        return sum(t.astype(jnp.float32) for t in terms[1:]) + terms[0].astype(jnp.float32)

    got = exchange(send, "panel", 1)
    per_row = cols * per_owner
    parts = [
        added(keep[s * per_row : (s + 1) * per_row], got[s * per_row : (s + 1) * per_row]).astype(jnp.bfloat16)
        for s in range(rows)
    ]
    got = [exchange(parts[s], "row", s) for s in range(1, rows)]
    parts = [
        added(*[p[s * per_owner : (s + 1) * per_owner] for p in [parts[0]] + got]).astype(jnp.bfloat16)
        for s in range(cols)
    ]
    got = [exchange(parts[s], "col", s) for s in range(1, cols)]
    mine = added(parts[0], *got).astype(jnp.bfloat16)
    line = jnp.stack([mine] + [exchange(mine, "col", s) for s in range(1, cols)])
    other = exchange(line, "panel", 1)
    smem = pl.BlockSpec(memory_space=pltpu.SMEM)
    vmem = pl.BlockSpec(memory_space=pltpu.VMEM)
    return pl.pallas_call(
        functools.partial(gradient_body, cols),
        out_shape=jax.ShapeDtypeStruct((layers * size, width), jnp.float32),
        in_specs=[smem, smem] + [vmem] * (2 + cols),
        out_specs=vmem,
        scratch_shapes=[pltpu.VMEM((cols,) + panel_tile.shape, jnp.bfloat16)],
        name="gradient",
    )(index, layer[None], line, other, *panels)


def solution(mesh):
    placed = (
        P(("row", "col", "panel"), None, None),
        P(("row", "col", "panel")),
        P(None, ("row", "col", "panel")),
        P(("row", "col", "panel"), None),
        P(("row", "col", "panel")),
        P("row", "col"),
        P("row", "col"),
        P("row", "col"),
        P("row", "col"),
    )
    return jax.shard_map(
        local, mesh=mesh, in_specs=placed, out_specs=P("row", ("col", "panel")), check_vma=False
    )
```

```python
import functools

import jax
import jax.numpy as jnp
from jax import lax
from jax.experimental import pallas as pl
from jax.experimental.pallas import tpu as pltpu
from jax.sharding import PartitionSpec as P


UNROLL = 4
WORDS = 8
VMEM_LIMIT = 28 * 1024 * 1024
VMEM_MARGIN = 4 * 1024 * 1024


def target(i, s, n):
    return i ^ s if n & (n - 1) == 0 else (i + s) % n


def source(i, s, n):
    return i ^ s if n & (n - 1) == 0 else (i - s) % n


def target_slot(i, j, n):
    return i ^ j if n & (n - 1) == 0 else (j - i) % n


def source_slot(i, j, n):
    return i ^ j if n & (n - 1) == 0 else (i - j) % n


def exchange(value, axis, slot):
    n = lax.axis_size(axis)
    return lax.ppermute(value, axis, [(i, target(i, slot, n)) for i in range(n)])


def masked_blocks(matrix, block_mask, block_size):
    mask_rows, mask_cols = block_mask.shape
    shaped = matrix.reshape(mask_rows, block_size, mask_cols, block_size)
    factor = block_mask.astype(matrix.dtype)[:, None, :, None]
    return (shaped * factor).reshape(mask_rows * block_size, mask_cols * block_size)


def place_of(sizes, per_owner, owner, block):
    rows, cols, layers = sizes
    far_layer = target_slot(lax.axis_index("panel"), owner % layers, layers)
    far_col = target_slot(lax.axis_index("col"), (owner // layers) % cols, cols)
    far_row = target_slot(lax.axis_index("row"), owner // (layers * cols), rows)
    near = far_row == 0
    at = jnp.where(near, far_layer, far_layer * (rows - 1) + far_row - 1)
    return near, (at * cols + far_col) * per_owner + block


def accumulate(chunk, table, basis, weighted, total):
    size = basis.shape[2]
    most = (table.shape[0] - 2 * WORDS) // (2 * WORDS)

    def step(i, carry):
        for j in range(UNROLL):
            at = (chunk * most + i * UNROLL + j) * WORDS
            rights = jnp.concatenate([weighted[table[at + 1]], weighted[table[at + 2]]], axis=1)
            found = lax.dot_general(
                basis[table[at]], rights, (((0,), (0,)), ((), ())), preferred_element_type=jnp.float32
            )
            total[table[at + 3]] += found[:, :size]
            total[table[at + 4]] += found[:, size:]
        return carry

    count = table[(2 * most + chunk) * WORDS]
    lax.fori_loop(0, (count + UNROLL - 1) // UNROLL, step, 0)


def clear(total):
    def zero(i, carry):
        total[i] = jnp.zeros(total.shape[1:], jnp.float32)
        return carry

    lax.fori_loop(0, total.shape[0], zero, 0)


def put(total, keep_ref, send_ref):
    half = keep_ref.shape[0]

    def one(i, carry):
        keep_ref[i] = total[i].astype(jnp.bfloat16)
        send_ref[i] = total[half + i].astype(jnp.bfloat16)
        return carry

    lax.fori_loop(0, half, one, 0)


def integrate_far_body(
    sizes, per_owner, trash, pair_ref, owner_ref, block_ref, basis_ref, pot_ref,
    weighted, table, keep_ref, send_ref, basis, pot_cols, total, pending, arrived,
):
    atoms, points, size = basis.shape
    parts = block_ref.shape[0]
    most = (table.shape[0] - 2 * WORDS) // (2 * WORDS)
    radix = pl.next_power_of_2(max(trash) + 1)

    def fetch(a):
        return pltpu.make_async_copy(basis_ref.at[a], basis.at[a], arrived.at[a])

    for a in range(atoms):
        fetch(a).start()
    for k in range(2 * atoms):
        pending[k] = -1
    clear(total)
    for k in range(points // size):
        row = pot_ref[k : k + 1, :]
        pot_cols[k * size : (k + 1) * size, :] = jnp.broadcast_to(row, (size, size)).T

    def unit(chunk, count, left, first, second, first_slot, second_slot):
        at = (jnp.where(chunk, most, 0) + count) * WORDS
        for k, word in enumerate((left, first, second, first_slot, second_slot)):
            table[at + k] = word

    def weigh_and_plan(a, counts):
        fetch(a).wait()
        for k in range(points // size):
            at = slice(k * size, (k + 1) * size)
            weighted[a, at, :] = (basis[a, at, :].astype(jnp.float32) * pot_cols[at, :]).astype(jnp.bfloat16)
        far_count, near_count = counts
        for k in range(parts // atoms):
            n = a * (parts // atoms) + k
            left, right = pair_ref[0, n], pair_ref[1, n]
            near, slot = place_of(sizes, per_owner, owner_ref[0, n], block_ref[n])
            key = left + jnp.where(near, atoms, 0)
            earlier = pending[key]
            fresh = earlier < 0
            pending[key] = jnp.where(fresh, right * radix + slot, -1)
            unit(near, jnp.where(near, near_count, far_count), left, earlier // radix, right, earlier % radix, slot)
            far_count += jnp.where(fresh | near, 0, 1)
            near_count += jnp.where(fresh | jnp.logical_not(near), 0, 1)
        return far_count, near_count

    counts = lax.fori_loop(0, atoms, weigh_and_plan, (jnp.int32(0), jnp.int32(0)))
    for chunk in range(2):

        def single(left, count):
            earlier = pending[chunk * atoms + left]
            right, slot = earlier // radix, earlier % radix
            unit(bool(chunk), count, left, right, right, slot, trash[chunk])
            return count + jnp.where(earlier < 0, 0, 1)

        count = lax.fori_loop(0, atoms, single, counts[chunk])
        for k in range(UNROLL - 1):
            unit(bool(chunk), count + k, 0, 0, 0, trash[chunk], trash[chunk])
        table[(2 * most + chunk) * WORDS] = count
    accumulate(0, table, basis, weighted, total)
    put(total, keep_ref, send_ref)


def integrate_near_body(table, basis, weighted, keep_ref, send_ref, total):
    clear(total)
    accumulate(1, table, basis, weighted, total)
    put(total, keep_ref, send_ref)


def integrate(basis_values, potential, pair_atoms, target_device, target_block, sizes, per_owner):
    atoms, points, size = basis_values.shape
    parts = target_block.shape[0]
    rows, cols, layers = sizes
    per_row = cols * per_owner
    trash = layers * (rows - 1) * per_row, layers * per_row
    most = (parts + atoms) // 2 + UNROLL + 1
    smem = pl.BlockSpec(memory_space=pltpu.SMEM)
    vmem = pl.BlockSpec(memory_space=pltpu.VMEM)

    def half(blocks):
        return jax.ShapeDtypeStruct((blocks // 2, size, size), jnp.bfloat16)

    def total(blocks):
        return pltpu.VMEM((blocks + 1, size, size), jnp.float32)

    def options(share):
        return dict(
            compiler_params=pltpu.CompilerParams(vmem_limit_bytes=VMEM_LIMIT),
            cost_estimate=pl.CostEstimate(
                flops=int(4 * parts * points * size * size * share),
                bytes_accessed=4 * basis_values.size,
                transcendentals=0,
            ),
        )

    weighted, table, far_keep, far_send = pl.pallas_call(
        functools.partial(integrate_far_body, sizes, per_owner, trash),
        out_shape=(
            jax.ShapeDtypeStruct(basis_values.shape, jnp.bfloat16),
            jax.ShapeDtypeStruct(((2 * most + 2) * WORDS,), jnp.int32),
            half(trash[0]),
            half(trash[0]),
        ),
        in_specs=[smem, smem, smem, pl.BlockSpec(memory_space=pltpu.HBM), vmem],
        out_specs=(vmem, smem, vmem, vmem),
        scratch_shapes=[
            pltpu.VMEM(basis_values.shape, jnp.bfloat16),
            pltpu.VMEM((points, size), jnp.float32),
            total(trash[0]),
            pltpu.SMEM((2 * atoms,), jnp.int32),
            pltpu.SemaphoreType.DMA((atoms,)),
        ],
        name="integrate_far",
        **options(1 - 1 / rows),
    )(
        pair_atoms,
        target_device.reshape(1, parts),
        target_block,
        pltpu.with_memory_space_constraint(basis_values, pltpu.HBM),
        potential.reshape(points // size, size),
    )
    near_keep, near_send = pl.pallas_call(
        integrate_near_body,
        out_shape=(half(trash[1]), half(trash[1])),
        in_specs=[smem, vmem, vmem],
        out_specs=(vmem, vmem),
        scratch_shapes=[total(trash[1])],
        name="integrate_near",
        **options(1 / rows),
    )(table, basis_values, weighted)
    return far_keep, far_send, near_keep, near_send


def index_of(row, col, s, count):
    return source_slot(row, source(col, s, count), count)


def product_body(count, *refs):
    lefts, rights, out = refs[:count], refs[count : 2 * count], refs[-2]
    stacked = refs[-1]
    for s in range(count):
        stacked[s] = rights[s][...]
    row, col = lax.axis_index("row"), lax.axis_index("col")
    found = None
    for s in range(count):
        term = jnp.dot(lefts[s][...], stacked[index_of(row, col, s, count)], preferred_element_type=jnp.float32)
        found = term if found is None else found + term
    out[...] = found.astype(out.dtype)


def product(lefts, rights, dtype):
    count = len(lefts)
    rows, columns = lefts[0].shape[0], rights[0].shape[1]
    vmem = pl.BlockSpec(memory_space=pltpu.VMEM)
    return pl.pallas_call(
        functools.partial(product_body, count),
        out_shape=jax.ShapeDtypeStruct((rows, columns), dtype),
        in_specs=[vmem] * (2 * count),
        out_specs=vmem,
        scratch_shapes=[pltpu.VMEM((count,) + rights[0].shape, rights[0].dtype)],
        cost_estimate=pl.CostEstimate(
            flops=2 * count * rows * columns * rights[0].shape[0],
            bytes_accessed=2 * count * (lefts[0].size + rights[0].size),
            transcendentals=0,
        ),
        compiler_params=pltpu.CompilerParams(vmem_limit_bytes=2 * VMEM_MARGIN),
        name="product",
    )(*lefts, *rights)


def gradient_body(count, own_ref, other_ref, *refs):
    rights, out, stacked = refs[:count], refs[-2], refs[-1]
    for s in range(count):
        stacked[s] = rights[s][...]
    blocks, size = own_ref.shape[1], own_ref.shape[2]
    row, col, side = lax.axis_index("row"), lax.axis_index("col"), lax.axis_index("panel")
    for which, ref in ((side, own_ref), (1 - side, other_ref)):
        found = None
        for s in range(count):
            left = jnp.concatenate([ref[s, b] for b in range(blocks)], axis=1)
            term = jnp.dot(left, stacked[index_of(row, col, s, count)], preferred_element_type=jnp.float32)
            found = term if found is None else found + term
        out[pl.ds(which * size, size), :] = found


def program(
    basis_values,
    potential,
    pair_atoms,
    target_device,
    target_block,
    density,
    density_mask,
    inverse_intersection,
    inverse_mask,
):
    size = basis_values.shape[2]
    rows, cols, layers = lax.axis_size("row"), lax.axis_size("col"), lax.axis_size("panel")
    layer = lax.axis_index("panel")
    tile_blocks = density_mask.shape[0]
    per_owner = tile_blocks // layers * tile_blocks

    width = inverse_intersection.shape[1] // layers
    mask_width = inverse_mask.shape[1] // layers
    density_used = masked_blocks(density, density_mask, size)
    inverse_used = masked_blocks(
        lax.dynamic_slice_in_dim(inverse_intersection, layer * width, width, 1),
        lax.dynamic_slice_in_dim(inverse_mask, layer * mask_width, mask_width, 1),
        size,
    )
    lefts = [density_used] + [exchange(density_used, "col", s) for s in range(1, cols)]
    rights = [inverse_used] + [exchange(inverse_used, "row", s) for s in range(1, rows)]

    far_keep, far_send, near_keep, near_send = integrate(
        basis_values, potential, pair_atoms, target_device, target_block, (rows, cols, layers), per_owner
    )

    panel_tile = product(lefts, rights, jnp.bfloat16)
    panels = [panel_tile] + [exchange(panel_tile, "row", s) for s in range(1, rows)]

    def added(*terms):
        return sum(t.astype(jnp.float32) for t in terms[1:]) + terms[0].astype(jnp.float32)

    per_row = cols * per_owner
    far_got = exchange(far_send, "panel", 1)
    near_got = exchange(near_send, "panel", 1)
    parts = [added(near_keep, near_got).astype(jnp.bfloat16)] + [
        added(far_keep[s * per_row : (s + 1) * per_row], far_got[s * per_row : (s + 1) * per_row]).astype(jnp.bfloat16)
        for s in range(rows - 1)
    ]
    got = [exchange(parts[s], "row", s) for s in range(1, rows)]
    parts = [
        added(*[p[s * per_owner : (s + 1) * per_owner] for p in [parts[0]] + got]).astype(jnp.bfloat16)
        for s in range(cols)
    ]
    got = [exchange(parts[s], "col", s) for s in range(1, cols)]
    mine = added(parts[0], *got).astype(jnp.bfloat16)
    line = jnp.stack([mine] + [exchange(mine, "col", s) for s in range(1, cols)])
    other = exchange(line, "panel", 1)
    vmem = pl.BlockSpec(memory_space=pltpu.VMEM)
    return pl.pallas_call(
        functools.partial(gradient_body, cols),
        out_shape=jax.ShapeDtypeStruct((layers * size, width), jnp.float32),
        in_specs=[vmem] * (2 + cols),
        out_specs=vmem,
        scratch_shapes=[pltpu.VMEM((cols,) + panel_tile.shape, jnp.bfloat16)],
        compiler_params=pltpu.CompilerParams(vmem_limit_bytes=2 * VMEM_MARGIN),
        name="gradient",
    )(line, other, *panels)


def solution(mesh):
    placed = (
        P(("row", "col", "panel"), None, None),
        P(("row", "col", "panel")),
        P(None, ("row", "col", "panel")),
        P(("row", "col", "panel"), None),
        P(("row", "col", "panel")),
        P("row", "col"),
        P("row", "col"),
        P("row", "col"),
        P("row", "col"),
    )
    return jax.shard_map(program, mesh=mesh, in_specs=placed, out_specs=P("row", ("col", "panel")), check_vma=False)
```

```python
import functools

import jax
import jax.numpy as jnp
from jax import lax
from jax.experimental import pallas as pl
from jax.experimental.pallas import tpu as pltpu
from jax.sharding import PartitionSpec as P


UNROLL = 4
VMEM_LIMIT = 36 * 1024 * 1024
VMEM_MARGIN = 4 * 1024 * 1024


def target(i, s, n):
    return i ^ s if n & (n - 1) == 0 else (i + s) % n


def source(i, s, n):
    return i ^ s if n & (n - 1) == 0 else (i - s) % n


def target_slot(i, j, n):
    return i ^ j if n & (n - 1) == 0 else (j - i) % n


def source_slot(i, j, n):
    return i ^ j if n & (n - 1) == 0 else (i - j) % n


def exchange(value, axis, slot):
    n = lax.axis_size(axis)
    return lax.ppermute(value, axis, [(i, target(i, slot, n)) for i in range(n)])


def masked_blocks(matrix, block_mask, block_size):
    mask_rows, mask_cols = block_mask.shape
    shaped = matrix.reshape(mask_rows, block_size, mask_cols, block_size)
    factor = block_mask.astype(matrix.dtype)[:, None, :, None]
    return (shaped * factor).reshape(mask_rows * block_size, mask_cols * block_size)


def place_of(sizes, per_owner, owner, block):
    rows, cols, layers = sizes
    far_layer = target_slot(lax.axis_index("panel"), owner % layers, layers)
    far_col = target_slot(lax.axis_index("col"), (owner // layers) % cols, cols)
    far_row = target_slot(lax.axis_index("row"), owner // (layers * cols), rows)
    near = (far_row == 0).astype(jnp.int32)
    at = jnp.where(near == 1, far_layer, far_layer * (rows - 1) + far_row - 1)
    return near, (at * cols + far_col) * per_owner + block + 1


def across(row):
    return jnp.broadcast_to(row, (row.shape[1], row.shape[1])).T


def most_units(parts, atoms):
    return (parts + atoms) // 2 + UNROLL


def plan(sizes, per_owner, atoms, radix, pairs, owner, block):
    parts = owner.shape[1]
    left, right = pairs[0:1, :], pairs[1:2, :]
    near, slot = place_of(sizes, per_owner, owner, block)
    key = left + near * atoms
    lane = lax.broadcasted_iota(jnp.int32, (parts, parts), 1)
    sublane = lax.broadcasted_iota(jnp.int32, (parts, parts), 0)
    earlier = (across(key) == key) & (sublane < lane)
    rank = jnp.sum(earlier.astype(jnp.int32), axis=0, keepdims=True)
    which = lax.broadcasted_iota(jnp.int32, (2 * atoms, parts), 0)
    members = jnp.sum((which == key).astype(jnp.int32), axis=1, keepdims=True)
    units = (members + 1) // 2
    before = (which < key) & ((which >= atoms) == (near == 1))
    start = jnp.sum(jnp.where(before, units, 0), axis=0, keepdims=True)
    entries = 2 * most_units(parts, atoms)
    at = 2 * start + rank + near * entries
    width = -(-(2 * entries + 2) // parts) * parts
    code = (left * radix + right) * radix + slot
    place = lax.broadcasted_iota(jnp.int32, (parts, width), 1)
    here = jnp.concatenate([across(at)] * (width // parts), axis=1) == place
    table = jnp.sum(jnp.where(here, jnp.concatenate([across(code)] * (width // parts), axis=1), 0), axis=0, keepdims=True)
    far_units = jnp.sum(jnp.where(which[:, 0:1] < atoms, units, 0), axis=0, keepdims=True)
    near_units = jnp.sum(jnp.where(which[:, 0:1] < atoms, 0, units), axis=0, keepdims=True)
    place = place[0:1, :]
    return jnp.where(place == width - 2, far_units, jnp.where(place == width - 1, near_units, table))


def accumulate(chunk, entries, radix, table, lefts, weighted, total):
    size = lefts.shape[1]

    def step(i, carry):
        for j in range(UNROLL):
            at = chunk * entries + 2 * (i * UNROLL + j)
            one, two = table[0, at], table[0, at + 1]
            rights = jnp.concatenate(
                [weighted[(one // radix) % radix], weighted[(two // radix) % radix]], axis=1
            )
            found = jnp.dot(lefts[one // (radix * radix)], rights, preferred_element_type=jnp.float32)
            total[one % radix] += found[:, :size]
            total[two % radix] += found[:, size:]
        return carry

    count = table[0, table.shape[1] - 2 + chunk]
    lax.fori_loop(0, (count + UNROLL - 1) // UNROLL, step, 0)


def clear(total):
    def zero(i, carry):
        total[i] = jnp.zeros(total.shape[1:], jnp.float32)
        return carry

    lax.fori_loop(0, total.shape[0], zero, 0)


def put(total, keep_ref, send_ref):
    half = keep_ref.shape[0]

    def one(i, carry):
        keep_ref[i] = total[i + 1].astype(jnp.bfloat16)
        send_ref[i] = total[half + i + 1].astype(jnp.bfloat16)
        return carry

    lax.fori_loop(0, half, one, 0)


def integrate_far_body(
    sizes, per_owner, entries, radix, pair_ref, owner_ref, block_ref, basis_ref, pot_ref,
    lefts, weighted, table_ref, keep_ref, send_ref,
    pairs, owner, block, pot, basis, pot_cols, total, table, small_sems, arrived,
):
    atoms, points, size = basis.shape
    small = [
        pltpu.make_async_copy(source_ref, to, small_sems.at[k])
        for k, (source_ref, to) in enumerate(
            ((pair_ref, pairs), (owner_ref, owner), (block_ref, block), (pot_ref, pot))
        )
    ]
    for copy in small:
        copy.start()

    def fetch(a):
        return pltpu.make_async_copy(basis_ref.at[a], basis.at[a], arrived.at[a])

    for a in range(atoms):
        fetch(a).start()
    clear(total)
    for copy in small:
        copy.wait()
    table_ref[...] = plan(sizes, per_owner, atoms, radix, pairs[...], owner[...], block[...])
    to_scalar = pltpu.make_async_copy(table_ref, table, small_sems.at[4])
    to_scalar.start()
    for k in range(points // size):
        pot_cols[k * size : (k + 1) * size, :] = across(pot[k : k + 1, :])

    def weigh(a, carry):
        fetch(a).wait()
        for k in range(points // size):
            at = slice(k * size, (k + 1) * size)
            values = basis[a, at, :]
            weighted[a, at, :] = (values.astype(jnp.float32) * pot_cols[at, :]).astype(jnp.bfloat16)
            lefts[a, :, at] = values.T
        return carry

    lax.fori_loop(0, atoms, weigh, 0)
    to_scalar.wait()
    accumulate(0, entries, radix, table, lefts, weighted, total)
    put(total, keep_ref, send_ref)


def integrate_near_body(entries, radix, table, lefts, weighted, keep_ref, send_ref, total):
    clear(total)
    accumulate(1, entries, radix, table, lefts, weighted, total)
    put(total, keep_ref, send_ref)


def integrate(basis_values, potential, pair_atoms, target_device, target_block, sizes, per_owner):
    atoms, points, size = basis_values.shape
    parts = target_block.shape[0]
    rows, cols, layers = sizes
    per_row = cols * per_owner
    far, near = layers * (rows - 1) * per_row, layers * per_row
    entries = 2 * most_units(parts, atoms)
    width = -(-(2 * entries + 2) // parts) * parts
    radix = pl.next_power_of_2(max(far + 1, near + 1, atoms))
    vmem = pl.BlockSpec(memory_space=pltpu.VMEM)
    hbm = pl.BlockSpec(memory_space=pltpu.HBM)

    def half(blocks):
        return jax.ShapeDtypeStruct((blocks // 2, size, size), jnp.bfloat16)

    def total(blocks):
        return pltpu.VMEM((blocks + 1, size, size), jnp.float32)

    def options(share):
        return dict(
            compiler_params=pltpu.CompilerParams(vmem_limit_bytes=VMEM_LIMIT),
            cost_estimate=pl.CostEstimate(
                flops=int(4 * parts * points * size * size * share),
                bytes_accessed=4 * basis_values.size,
                transcendentals=0,
            ),
        )

    def in_hbm(array):
        return pltpu.with_memory_space_constraint(array, pltpu.HBM)

    lefts, weighted, table, far_keep, far_send = pl.pallas_call(
        functools.partial(integrate_far_body, sizes, per_owner, entries, radix),
        out_shape=(
            jax.ShapeDtypeStruct((atoms, size, points), jnp.bfloat16),
            jax.ShapeDtypeStruct((atoms, points, size), jnp.bfloat16),
            jax.ShapeDtypeStruct((1, width), jnp.int32),
            half(far),
            half(far),
        ),
        in_specs=[hbm] * 5,
        out_specs=(vmem,) * 5,
        scratch_shapes=[
            pltpu.VMEM((2, parts), jnp.int32),
            pltpu.VMEM((1, parts), jnp.int32),
            pltpu.VMEM((1, parts), jnp.int32),
            pltpu.VMEM((points // size, size), jnp.float32),
            pltpu.VMEM((atoms, points, size), jnp.bfloat16),
            pltpu.VMEM((points, size), jnp.float32),
            total(far),
            pltpu.SMEM((1, width), jnp.int32),
            pltpu.SemaphoreType.DMA((5,)),
            pltpu.SemaphoreType.DMA((atoms,)),
        ],
        name="integrate_far",
        **options(1 - 1 / rows),
    )(
        in_hbm(pair_atoms),
        in_hbm(target_device.reshape(1, parts)),
        in_hbm(target_block.reshape(1, parts)),
        in_hbm(basis_values),
        in_hbm(potential.reshape(points // size, size)),
    )
    near_keep, near_send = pl.pallas_call(
        functools.partial(integrate_near_body, entries, radix),
        out_shape=(half(near), half(near)),
        in_specs=[pl.BlockSpec(memory_space=pltpu.SMEM), vmem, vmem],
        out_specs=(vmem, vmem),
        scratch_shapes=[total(near)],
        name="integrate_near",
        **options(1 / rows),
    )(table, lefts, weighted)
    return far_keep, far_send, near_keep, near_send


def index_of(row, col, s, count):
    return source_slot(row, source(col, s, count), count)


def product_body(count, *refs):
    lefts, rights, out = refs[:count], refs[count : 2 * count], refs[-2]
    stacked = refs[-1]
    for s in range(count):
        stacked[s] = rights[s][...]
    row, col = lax.axis_index("row"), lax.axis_index("col")
    found = None
    for s in range(count):
        term = jnp.dot(lefts[s][...], stacked[index_of(row, col, s, count)], preferred_element_type=jnp.float32)
        found = term if found is None else found + term
    out[...] = found.astype(out.dtype)


def product(lefts, rights, dtype):
    count = len(lefts)
    rows, columns = lefts[0].shape[0], rights[0].shape[1]
    vmem = pl.BlockSpec(memory_space=pltpu.VMEM)
    return pl.pallas_call(
        functools.partial(product_body, count),
        out_shape=jax.ShapeDtypeStruct((rows, columns), dtype),
        in_specs=[vmem] * (2 * count),
        out_specs=vmem,
        scratch_shapes=[pltpu.VMEM((count,) + rights[0].shape, rights[0].dtype)],
        cost_estimate=pl.CostEstimate(
            flops=2 * count * rows * columns * rights[0].shape[0],
            bytes_accessed=2 * count * (lefts[0].size + rights[0].size),
            transcendentals=0,
        ),
        compiler_params=pltpu.CompilerParams(vmem_limit_bytes=2 * VMEM_MARGIN),
        name="product",
    )(*lefts, *rights)


def gradient_body(count, own_ref, other_ref, *refs):
    rights, out, stacked = refs[:count], refs[-2], refs[-1]
    for s in range(count):
        stacked[s] = rights[s][...]
    blocks, size = own_ref.shape[1], own_ref.shape[2]
    row, col, side = lax.axis_index("row"), lax.axis_index("col"), lax.axis_index("panel")
    for which, ref in ((side, own_ref), (1 - side, other_ref)):
        found = None
        for s in range(count):
            left = jnp.concatenate([ref[s, b] for b in range(blocks)], axis=1)
            term = jnp.dot(left, stacked[index_of(row, col, s, count)], preferred_element_type=jnp.float32)
            found = term if found is None else found + term
        out[pl.ds(which * size, size), :] = found


def program(
    basis_values,
    potential,
    pair_atoms,
    target_device,
    target_block,
    density,
    density_mask,
    inverse_intersection,
    inverse_mask,
):
    size = basis_values.shape[2]
    rows, cols, layers = lax.axis_size("row"), lax.axis_size("col"), lax.axis_size("panel")
    layer = lax.axis_index("panel")
    tile_blocks = density_mask.shape[0]
    per_owner = tile_blocks // layers * tile_blocks

    width = inverse_intersection.shape[1] // layers
    mask_width = inverse_mask.shape[1] // layers
    density_used = masked_blocks(density, density_mask, size)
    inverse_used = masked_blocks(
        lax.dynamic_slice_in_dim(inverse_intersection, layer * width, width, 1),
        lax.dynamic_slice_in_dim(inverse_mask, layer * mask_width, mask_width, 1),
        size,
    )
    lefts = [density_used] + [exchange(density_used, "col", s) for s in range(1, cols)]
    rights = [inverse_used] + [exchange(inverse_used, "row", s) for s in range(1, rows)]

    far_keep, far_send, near_keep, near_send = integrate(
        basis_values, potential, pair_atoms, target_device, target_block, (rows, cols, layers), per_owner
    )

    panel_tile = product(lefts, rights, jnp.bfloat16)
    panels = [panel_tile] + [exchange(panel_tile, "row", s) for s in range(1, rows)]

    def added(*terms):
        return sum(t.astype(jnp.float32) for t in terms[1:]) + terms[0].astype(jnp.float32)

    per_row = cols * per_owner
    far_got = exchange(far_send, "panel", 1)
    near_got = exchange(near_send, "panel", 1)
    parts = [added(near_keep, near_got).astype(jnp.bfloat16)] + [
        added(far_keep[s * per_row : (s + 1) * per_row], far_got[s * per_row : (s + 1) * per_row]).astype(jnp.bfloat16)
        for s in range(rows - 1)
    ]
    got = [exchange(parts[s], "row", s) for s in range(1, rows)]
    parts = [
        added(*[p[s * per_owner : (s + 1) * per_owner] for p in [parts[0]] + got]).astype(jnp.bfloat16)
        for s in range(cols)
    ]
    got = [exchange(parts[s], "col", s) for s in range(1, cols)]
    mine = added(parts[0], *got).astype(jnp.bfloat16)
    line = jnp.stack([mine] + [exchange(mine, "col", s) for s in range(1, cols)])
    other = exchange(line, "panel", 1)
    vmem = pl.BlockSpec(memory_space=pltpu.VMEM)
    return pl.pallas_call(
        functools.partial(gradient_body, cols),
        out_shape=jax.ShapeDtypeStruct((layers * size, width), jnp.float32),
        in_specs=[vmem] * (2 + cols),
        out_specs=vmem,
        scratch_shapes=[pltpu.VMEM((cols,) + panel_tile.shape, jnp.bfloat16)],
        compiler_params=pltpu.CompilerParams(vmem_limit_bytes=2 * VMEM_MARGIN),
        name="gradient",
    )(line, other, *panels)


def solution(mesh):
    placed = (
        P(("row", "col", "panel"), None, None),
        P(("row", "col", "panel")),
        P(None, ("row", "col", "panel")),
        P(("row", "col", "panel"), None),
        P(("row", "col", "panel")),
        P("row", "col"),
        P("row", "col"),
        P("row", "col"),
        P("row", "col"),
    )
    return jax.shard_map(program, mesh=mesh, in_specs=placed, out_specs=P("row", ("col", "panel")), check_vma=False)
```

```python
import functools

import jax
import jax.numpy as jnp
from jax import lax
from jax.experimental import pallas as pl
from jax.experimental.pallas import tpu as pltpu
from jax.sharding import PartitionSpec as P


UNROLL = 8
IN_FLIGHT = 6
VMEM_LIMIT = 36 * 1024 * 1024
VMEM_MARGIN = 4 * 1024 * 1024


def target(i, s, n):
    return i ^ s if n & (n - 1) == 0 else (i + s) % n


def source(i, s, n):
    return i ^ s if n & (n - 1) == 0 else (i - s) % n


def target_slot(i, j, n):
    return i ^ j if n & (n - 1) == 0 else (j - i) % n


def source_slot(i, j, n):
    return i ^ j if n & (n - 1) == 0 else (i - j) % n


def exchange(value, axis, slot):
    n = lax.axis_size(axis)
    return lax.ppermute(value, axis, [(i, target(i, slot, n)) for i in range(n)])


def masked_blocks(matrix, block_mask, block_size):
    mask_rows, mask_cols = block_mask.shape
    shaped = matrix.reshape(mask_rows, block_size, mask_cols, block_size)
    factor = block_mask.astype(matrix.dtype)[:, None, :, None]
    return (shaped * factor).reshape(mask_rows * block_size, mask_cols * block_size)


def place_of(sizes, per_owner, owner, block):
    rows, cols, layers = sizes
    far_layer = target_slot(lax.axis_index("panel"), owner % layers, layers)
    far_col = target_slot(lax.axis_index("col"), (owner // layers) % cols, cols)
    far_row = target_slot(lax.axis_index("row"), owner // (layers * cols), rows)
    near = (far_row == 0).astype(jnp.int32)
    at = jnp.where(near == 1, far_layer, far_layer * (rows - 1) + far_row - 1)
    return near, (at * cols + far_col) * per_owner + block + 1


def across(row):
    return jnp.broadcast_to(row, (row.shape[1], row.shape[1])).T


def most_units(parts, atoms):
    return (parts + atoms) // 2 + UNROLL


def plan(sizes, per_owner, atoms, radix, pairs, owner, block):
    parts = owner.shape[1]
    left, right = pairs[0:1, :], pairs[1:2, :]
    near, slot = place_of(sizes, per_owner, owner, block)
    key = left + near * atoms
    lane = lax.broadcasted_iota(jnp.int32, (parts, parts), 1)
    sublane = lax.broadcasted_iota(jnp.int32, (parts, parts), 0)
    earlier = (across(key) == key) & (sublane < lane)
    rank = jnp.sum(earlier.astype(jnp.int32), axis=0, keepdims=True)
    which = lax.broadcasted_iota(jnp.int32, (2 * atoms, parts), 0)
    members = jnp.sum((which == key).astype(jnp.int32), axis=1, keepdims=True)
    units = (members + 1) // 2
    before = (which < key) & ((which >= atoms) == (near == 1))
    start = jnp.sum(jnp.where(before, units, 0), axis=0, keepdims=True)
    entries = 2 * most_units(parts, atoms)
    at = 2 * start + rank + near * entries
    width = -(-(2 * entries + 2) // parts) * parts
    code = (left * radix + right) * radix + slot
    place = lax.broadcasted_iota(jnp.int32, (parts, width), 1)
    here = jnp.concatenate([across(at)] * (width // parts), axis=1) == place
    table = jnp.sum(jnp.where(here, jnp.concatenate([across(code)] * (width // parts), axis=1), 0), axis=0, keepdims=True)
    far_units = jnp.sum(jnp.where(which[:, 0:1] < atoms, units, 0), axis=0, keepdims=True)
    near_units = jnp.sum(jnp.where(which[:, 0:1] < atoms, 0, units), axis=0, keepdims=True)
    place = place[0:1, :]
    return jnp.where(place == width - 2, far_units, jnp.where(place == width - 1, near_units, table))


def accumulate(chunk, entries, radix, table, lefts, weighted, total):
    size = lefts.shape[1]

    def step(i, carry):
        for j in range(UNROLL):
            at = chunk * entries + 2 * (i * UNROLL + j)
            one, two = table[0, at], table[0, at + 1]
            rights = jnp.concatenate(
                [weighted[(one // radix) % radix], weighted[(two // radix) % radix]], axis=1
            )
            found = jnp.dot(lefts[one // (radix * radix)], rights, preferred_element_type=jnp.float32)
            total[one % radix] += found[:, :size]
            total[two % radix] += found[:, size:]
        return carry

    count = table[0, table.shape[1] - 2 + chunk]
    lax.fori_loop(0, (count + UNROLL - 1) // UNROLL, step, 0)


def clear(total):
    def zero(i, carry):
        total[i] = jnp.zeros(total.shape[1:], jnp.float32)
        return carry

    lax.fori_loop(0, total.shape[0], zero, 0)


def put(total, keep_ref, send_ref):
    half = keep_ref.shape[0]

    def one(i, carry):
        keep_ref[i] = total[i + 1].astype(jnp.bfloat16)
        send_ref[i] = total[half + i + 1].astype(jnp.bfloat16)
        return carry

    lax.fori_loop(0, half, one, 0)


def integrate_far_body(
    sizes, per_owner, entries, radix, pair_ref, owner_ref, block_ref, basis_ref, pot_ref,
    lefts, weighted, table_ref, keep_ref, send_ref,
    pairs, owner, block, pot, basis, pot_cols, total, table, small_sems, arrived,
):
    atoms, points, size = basis.shape
    small = [
        pltpu.make_async_copy(source_ref, to, small_sems.at[k])
        for k, (source_ref, to) in enumerate(
            ((pair_ref, pairs), (owner_ref, owner), (block_ref, block), (pot_ref, pot))
        )
    ]
    for copy in small:
        copy.start()

    def fetch(a):
        return pltpu.make_async_copy(basis_ref.at[a], basis.at[a], arrived.at[a])

    for a in range(IN_FLIGHT):
        fetch(a).start()
    clear(total)
    for copy in small:
        copy.wait()
    table_ref[...] = plan(sizes, per_owner, atoms, radix, pairs[...], owner[...], block[...])
    to_scalar = pltpu.make_async_copy(table_ref, table, small_sems.at[4])
    to_scalar.start()
    for k in range(points // size):
        pot_cols[k * size : (k + 1) * size, :] = across(pot[k : k + 1, :])

    def weigh(a, carry):
        fetch(a).wait()

        @pl.when(a + IN_FLIGHT < atoms)
        def _():
            fetch(a + IN_FLIGHT).start()

        for k in range(points // size):
            at = slice(k * size, (k + 1) * size)
            values = basis[a, at, :]
            weighted[a, at, :] = (values.astype(jnp.float32) * pot_cols[at, :]).astype(jnp.bfloat16)
            lefts[a, :, at] = values.T
        return carry

    lax.fori_loop(0, atoms, weigh, 0)
    to_scalar.wait()
    accumulate(0, entries, radix, table, lefts, weighted, total)
    put(total, keep_ref, send_ref)


def integrate_near_body(entries, radix, table, lefts, weighted, keep_ref, send_ref, total):
    clear(total)
    accumulate(1, entries, radix, table, lefts, weighted, total)
    put(total, keep_ref, send_ref)


def integrate(basis_values, potential, pair_atoms, target_device, target_block, sizes, per_owner):
    atoms, points, size = basis_values.shape
    parts = target_block.shape[0]
    rows, cols, layers = sizes
    per_row = cols * per_owner
    far, near = layers * (rows - 1) * per_row, layers * per_row
    entries = 2 * most_units(parts, atoms)
    width = -(-(2 * entries + 2) // parts) * parts
    radix = pl.next_power_of_2(max(far + 1, near + 1, atoms))
    vmem = pl.BlockSpec(memory_space=pltpu.VMEM)
    hbm = pl.BlockSpec(memory_space=pltpu.HBM)

    def half(blocks):
        return jax.ShapeDtypeStruct((blocks // 2, size, size), jnp.bfloat16)

    def total(blocks):
        return pltpu.VMEM((blocks + 1, size, size), jnp.float32)

    def options(share):
        return dict(
            compiler_params=pltpu.CompilerParams(vmem_limit_bytes=VMEM_LIMIT),
            cost_estimate=pl.CostEstimate(
                flops=int(4 * parts * points * size * size * share),
                bytes_accessed=4 * basis_values.size,
                transcendentals=0,
            ),
        )

    def in_hbm(array):
        return pltpu.with_memory_space_constraint(array, pltpu.HBM)

    lefts, weighted, table, far_keep, far_send = pl.pallas_call(
        functools.partial(integrate_far_body, sizes, per_owner, entries, radix),
        out_shape=(
            jax.ShapeDtypeStruct((atoms, size, points), jnp.bfloat16),
            jax.ShapeDtypeStruct((atoms, points, size), jnp.bfloat16),
            jax.ShapeDtypeStruct((1, width), jnp.int32),
            half(far),
            half(far),
        ),
        in_specs=[hbm] * 5,
        out_specs=(vmem,) * 5,
        scratch_shapes=[
            pltpu.VMEM((2, parts), jnp.int32),
            pltpu.VMEM((1, parts), jnp.int32),
            pltpu.VMEM((1, parts), jnp.int32),
            pltpu.VMEM((points // size, size), jnp.float32),
            pltpu.VMEM((atoms, points, size), jnp.bfloat16),
            pltpu.VMEM((points, size), jnp.float32),
            total(far),
            pltpu.SMEM((1, width), jnp.int32),
            pltpu.SemaphoreType.DMA((5,)),
            pltpu.SemaphoreType.DMA((atoms,)),
        ],
        name="integrate_far",
        **options(1 - 1 / rows),
    )(
        in_hbm(pair_atoms),
        in_hbm(target_device.reshape(1, parts)),
        in_hbm(target_block.reshape(1, parts)),
        in_hbm(basis_values),
        in_hbm(potential.reshape(points // size, size)),
    )
    near_keep, near_send = pl.pallas_call(
        functools.partial(integrate_near_body, entries, radix),
        out_shape=(half(near), half(near)),
        in_specs=[pl.BlockSpec(memory_space=pltpu.SMEM), vmem, vmem],
        out_specs=(vmem, vmem),
        scratch_shapes=[total(near)],
        name="integrate_near",
        **options(1 / rows),
    )(table, lefts, weighted)
    return far_keep, far_send, near_keep, near_send


def index_of(row, col, s, count):
    return source_slot(row, source(col, s, count), count)


def product_body(count, *refs):
    lefts, rights, out = refs[:count], refs[count : 2 * count], refs[-2]
    stacked = refs[-1]
    for s in range(count):
        stacked[s] = rights[s][...]
    row, col = lax.axis_index("row"), lax.axis_index("col")
    found = None
    for s in range(count):
        term = jnp.dot(lefts[s][...], stacked[index_of(row, col, s, count)], preferred_element_type=jnp.float32)
        found = term if found is None else found + term
    out[...] = found.astype(out.dtype)


def product(lefts, rights, dtype):
    count = len(lefts)
    rows, columns = lefts[0].shape[0], rights[0].shape[1]
    vmem = pl.BlockSpec(memory_space=pltpu.VMEM)
    return pl.pallas_call(
        functools.partial(product_body, count),
        out_shape=jax.ShapeDtypeStruct((rows, columns), dtype),
        in_specs=[vmem] * (2 * count),
        out_specs=vmem,
        scratch_shapes=[pltpu.VMEM((count,) + rights[0].shape, rights[0].dtype)],
        cost_estimate=pl.CostEstimate(
            flops=2 * count * rows * columns * rights[0].shape[0],
            bytes_accessed=2 * count * (lefts[0].size + rights[0].size),
            transcendentals=0,
        ),
        compiler_params=pltpu.CompilerParams(vmem_limit_bytes=2 * VMEM_MARGIN),
        name="product",
    )(*lefts, *rights)


def gradient_body(count, own_ref, other_ref, *refs):
    rights, out, stacked = refs[:count], refs[-2], refs[-1]
    for s in range(count):
        stacked[s] = rights[s][...]
    blocks, size = own_ref.shape[1], own_ref.shape[2]
    row, col, side = lax.axis_index("row"), lax.axis_index("col"), lax.axis_index("panel")
    for which, ref in ((side, own_ref), (1 - side, other_ref)):
        found = None
        for s in range(count):
            left = jnp.concatenate([ref[s, b] for b in range(blocks)], axis=1)
            term = jnp.dot(left, stacked[index_of(row, col, s, count)], preferred_element_type=jnp.float32)
            found = term if found is None else found + term
        out[pl.ds(which * size, size), :] = found


def program(
    basis_values,
    potential,
    pair_atoms,
    target_device,
    target_block,
    density,
    density_mask,
    inverse_intersection,
    inverse_mask,
):
    size = basis_values.shape[2]
    rows, cols, layers = lax.axis_size("row"), lax.axis_size("col"), lax.axis_size("panel")
    layer = lax.axis_index("panel")
    tile_blocks = density_mask.shape[0]
    per_owner = tile_blocks // layers * tile_blocks

    width = inverse_intersection.shape[1] // layers
    mask_width = inverse_mask.shape[1] // layers
    density_used = masked_blocks(density, density_mask, size)
    inverse_used = masked_blocks(
        lax.dynamic_slice_in_dim(inverse_intersection, layer * width, width, 1),
        lax.dynamic_slice_in_dim(inverse_mask, layer * mask_width, mask_width, 1),
        size,
    )
    lefts = [density_used] + [exchange(density_used, "col", s) for s in range(1, cols)]
    rights = [inverse_used] + [exchange(inverse_used, "row", s) for s in range(1, rows)]

    far_keep, far_send, near_keep, near_send = integrate(
        basis_values, potential, pair_atoms, target_device, target_block, (rows, cols, layers), per_owner
    )

    panel_tile = product(lefts, rights, jnp.bfloat16)
    panels = [panel_tile] + [exchange(panel_tile, "row", s) for s in range(1, rows)]

    def added(*terms):
        return sum(t.astype(jnp.float32) for t in terms[1:]) + terms[0].astype(jnp.float32)

    per_row = cols * per_owner
    far_got = exchange(far_send, "panel", 1)
    near_got = exchange(near_send, "panel", 1)
    parts = [added(near_keep, near_got).astype(jnp.bfloat16)] + [
        added(far_keep[s * per_row : (s + 1) * per_row], far_got[s * per_row : (s + 1) * per_row]).astype(jnp.bfloat16)
        for s in range(rows - 1)
    ]
    got = [exchange(parts[s], "row", s) for s in range(1, rows)]
    parts = [
        added(*[p[s * per_owner : (s + 1) * per_owner] for p in [parts[0]] + got]).astype(jnp.bfloat16)
        for s in range(cols)
    ]
    got = [exchange(parts[s], "col", s) for s in range(1, cols)]
    mine = added(parts[0], *got).astype(jnp.bfloat16)
    line = jnp.stack([mine] + [exchange(mine, "col", s) for s in range(1, cols)])
    other = exchange(line, "panel", 1)
    vmem = pl.BlockSpec(memory_space=pltpu.VMEM)
    return pl.pallas_call(
        functools.partial(gradient_body, cols),
        out_shape=jax.ShapeDtypeStruct((layers * size, width), jnp.float32),
        in_specs=[vmem] * (2 + cols),
        out_specs=vmem,
        scratch_shapes=[pltpu.VMEM((cols,) + panel_tile.shape, jnp.bfloat16)],
        compiler_params=pltpu.CompilerParams(vmem_limit_bytes=2 * VMEM_MARGIN),
        name="gradient",
    )(line, other, *panels)


def solution(mesh):
    placed = (
        P(("row", "col", "panel"), None, None),
        P(("row", "col", "panel")),
        P(None, ("row", "col", "panel")),
        P(("row", "col", "panel"), None),
        P(("row", "col", "panel")),
        P("row", "col"),
        P("row", "col"),
        P("row", "col"),
        P("row", "col"),
    )
    return jax.shard_map(program, mesh=mesh, in_specs=placed, out_specs=P("row", ("col", "panel")), check_vma=False)
```

```python
import functools

import jax
import jax.numpy as jnp
from jax import lax
from jax.experimental import pallas as pl
from jax.experimental.pallas import tpu as pltpu
from jax.sharding import PartitionSpec as P


UNROLL = 8
REST = 2
IN_FLIGHT = 6
VMEM_LIMIT = 36 * 1024 * 1024
VMEM_MARGIN = 4 * 1024 * 1024


def target(i, s, n):
    return i ^ s if n & (n - 1) == 0 else (i + s) % n


def source(i, s, n):
    return i ^ s if n & (n - 1) == 0 else (i - s) % n


def target_slot(i, j, n):
    return i ^ j if n & (n - 1) == 0 else (j - i) % n


def source_slot(i, j, n):
    return i ^ j if n & (n - 1) == 0 else (i - j) % n


def exchange(value, axis, slot):
    n = lax.axis_size(axis)
    return lax.ppermute(value, axis, [(i, target(i, slot, n)) for i in range(n)])


def masked_blocks(matrix, block_mask, block_size):
    mask_rows, mask_cols = block_mask.shape
    shaped = matrix.reshape(mask_rows, block_size, mask_cols, block_size)
    factor = block_mask.astype(matrix.dtype)[:, None, :, None]
    return (shaped * factor).reshape(mask_rows * block_size, mask_cols * block_size)


def place_of(sizes, per_owner, owner, block):
    rows, cols, layers = sizes
    far_layer = target_slot(lax.axis_index("panel"), owner % layers, layers)
    far_col = target_slot(lax.axis_index("col"), (owner // layers) % cols, cols)
    far_row = target_slot(lax.axis_index("row"), owner // (layers * cols), rows)
    near = (far_row == 0).astype(jnp.int32)
    at = jnp.where(near == 1, far_layer, far_layer * (rows - 1) + far_row - 1)
    return near, (at * cols + far_col) * per_owner + block + 1


def across(row):
    return jnp.broadcast_to(row, (row.shape[1], row.shape[1])).T


def most_units(parts, atoms):
    return (parts + atoms) // 2 + UNROLL


def plan(sizes, per_owner, atoms, radix, pairs, owner, block):
    parts = owner.shape[1]
    left, right = pairs[0:1, :], pairs[1:2, :]
    near, slot = place_of(sizes, per_owner, owner, block)
    key = left + near * atoms
    lane = lax.broadcasted_iota(jnp.int32, (parts, parts), 1)
    sublane = lax.broadcasted_iota(jnp.int32, (parts, parts), 0)
    earlier = (across(key) == key) & (sublane < lane)
    rank = jnp.sum(earlier.astype(jnp.int32), axis=0, keepdims=True)
    which = lax.broadcasted_iota(jnp.int32, (2 * atoms, parts), 0)
    members = jnp.sum((which == key).astype(jnp.int32), axis=1, keepdims=True)
    units = (members + 1) // 2
    before = (which < key) & ((which >= atoms) == (near == 1))
    start = jnp.sum(jnp.where(before, units, 0), axis=0, keepdims=True)
    entries = 2 * most_units(parts, atoms)
    at = 2 * start + rank + near * entries
    width = -(-(2 * entries + 2) // parts) * parts
    code = (left * radix + right) * radix + slot
    place = lax.broadcasted_iota(jnp.int32, (parts, width), 1)
    here = jnp.concatenate([across(at)] * (width // parts), axis=1) == place
    table = jnp.sum(jnp.where(here, jnp.concatenate([across(code)] * (width // parts), axis=1), 0), axis=0, keepdims=True)
    far_units = jnp.sum(jnp.where(which[:, 0:1] < atoms, units, 0), axis=0, keepdims=True)
    near_units = jnp.sum(jnp.where(which[:, 0:1] < atoms, 0, units), axis=0, keepdims=True)
    place = place[0:1, :]
    return jnp.where(place == width - 2, far_units, jnp.where(place == width - 1, near_units, table))


def accumulate(chunk, entries, radix, table, lefts, weighted, total):
    size = lefts.shape[1]

    def units(first, number):
        for j in range(number):
            at = chunk * entries + 2 * (first + j)
            one, two = table[0, at], table[0, at + 1]
            rights = jnp.concatenate(
                [weighted[(one // radix) % radix], weighted[(two // radix) % radix]], axis=1
            )
            found = jnp.dot(lefts[one // (radix * radix)], rights, preferred_element_type=jnp.float32)
            total[one % radix] += found[:, :size]
            total[two % radix] += found[:, size:]

    def many(i, carry):
        units(i * UNROLL, UNROLL)
        return carry

    def few(i, carry):
        units(whole * UNROLL + i * REST, REST)
        return carry

    count = table[0, table.shape[1] - 2 + chunk]
    whole = count // UNROLL
    lax.fori_loop(0, whole, many, 0)
    lax.fori_loop(0, (count - whole * UNROLL + REST - 1) // REST, few, 0)


def clear(total):
    def zero(i, carry):
        total[i] = jnp.zeros(total.shape[1:], jnp.float32)
        return carry

    lax.fori_loop(0, total.shape[0], zero, 0)


def put(total, keep_ref, send_ref):
    half = keep_ref.shape[0]

    def one(i, carry):
        keep_ref[i] = total[i + 1].astype(jnp.bfloat16)
        send_ref[i] = total[half + i + 1].astype(jnp.bfloat16)
        return carry

    lax.fori_loop(0, half, one, 0)


def integrate_far_body(
    sizes, per_owner, entries, radix, pair_ref, owner_ref, block_ref, basis_ref, pot_ref,
    lefts, weighted, table_ref, keep_ref, send_ref,
    pairs, owner, block, pot, basis, pot_cols, total, table, small_sems, arrived,
):
    atoms, points, size = basis.shape
    small = [
        pltpu.make_async_copy(source_ref, to, small_sems.at[k])
        for k, (source_ref, to) in enumerate(
            ((pair_ref, pairs), (owner_ref, owner), (block_ref, block), (pot_ref, pot))
        )
    ]
    for copy in small:
        copy.start()

    def fetch(a):
        return pltpu.make_async_copy(basis_ref.at[a], basis.at[a], arrived.at[a])

    for a in range(IN_FLIGHT):
        fetch(a).start()
    clear(total)
    for copy in small:
        copy.wait()
    table_ref[...] = plan(sizes, per_owner, atoms, radix, pairs[...], owner[...], block[...])
    to_scalar = pltpu.make_async_copy(table_ref, table, small_sems.at[4])
    to_scalar.start()
    for k in range(points // size):
        pot_cols[k * size : (k + 1) * size, :] = across(pot[k : k + 1, :])

    def weigh(a, carry):
        fetch(a).wait()

        @pl.when(a + IN_FLIGHT < atoms)
        def _():
            fetch(a + IN_FLIGHT).start()

        for k in range(points // size):
            at = slice(k * size, (k + 1) * size)
            values = basis[a, at, :]
            weighted[a, at, :] = (values.astype(jnp.float32) * pot_cols[at, :]).astype(jnp.bfloat16)
            lefts[a, :, at] = values.T
        return carry

    lax.fori_loop(0, atoms, weigh, 0)
    to_scalar.wait()
    accumulate(0, entries, radix, table, lefts, weighted, total)
    put(total, keep_ref, send_ref)


def integrate_near_body(entries, radix, table, lefts, weighted, keep_ref, send_ref, total):
    clear(total)
    accumulate(1, entries, radix, table, lefts, weighted, total)
    put(total, keep_ref, send_ref)


def integrate(basis_values, potential, pair_atoms, target_device, target_block, sizes, per_owner):
    atoms, points, size = basis_values.shape
    parts = target_block.shape[0]
    rows, cols, layers = sizes
    per_row = cols * per_owner
    far, near = layers * (rows - 1) * per_row, layers * per_row
    entries = 2 * most_units(parts, atoms)
    width = -(-(2 * entries + 2) // parts) * parts
    radix = pl.next_power_of_2(max(far + 1, near + 1, atoms))
    vmem = pl.BlockSpec(memory_space=pltpu.VMEM)
    hbm = pl.BlockSpec(memory_space=pltpu.HBM)

    def half(blocks):
        return jax.ShapeDtypeStruct((blocks // 2, size, size), jnp.bfloat16)

    def total(blocks):
        return pltpu.VMEM((blocks + 1, size, size), jnp.float32)

    def options(share):
        return dict(
            compiler_params=pltpu.CompilerParams(vmem_limit_bytes=VMEM_LIMIT),
            cost_estimate=pl.CostEstimate(
                flops=int(4 * parts * points * size * size * share),
                bytes_accessed=4 * basis_values.size,
                transcendentals=0,
            ),
        )

    def in_hbm(array):
        return pltpu.with_memory_space_constraint(array, pltpu.HBM)

    lefts, weighted, table, far_keep, far_send = pl.pallas_call(
        functools.partial(integrate_far_body, sizes, per_owner, entries, radix),
        out_shape=(
            jax.ShapeDtypeStruct((atoms, size, points), jnp.bfloat16),
            jax.ShapeDtypeStruct((atoms, points, size), jnp.bfloat16),
            jax.ShapeDtypeStruct((1, width), jnp.int32),
            half(far),
            half(far),
        ),
        in_specs=[hbm] * 5,
        out_specs=(vmem,) * 5,
        scratch_shapes=[
            pltpu.VMEM((2, parts), jnp.int32),
            pltpu.VMEM((1, parts), jnp.int32),
            pltpu.VMEM((1, parts), jnp.int32),
            pltpu.VMEM((points // size, size), jnp.float32),
            pltpu.VMEM((atoms, points, size), jnp.bfloat16),
            pltpu.VMEM((points, size), jnp.float32),
            total(far),
            pltpu.SMEM((1, width), jnp.int32),
            pltpu.SemaphoreType.DMA((5,)),
            pltpu.SemaphoreType.DMA((atoms,)),
        ],
        name="integrate_far",
        **options(1 - 1 / rows),
    )(
        in_hbm(pair_atoms),
        in_hbm(target_device.reshape(1, parts)),
        in_hbm(target_block.reshape(1, parts)),
        in_hbm(basis_values),
        in_hbm(potential.reshape(points // size, size)),
    )
    near_keep, near_send = pl.pallas_call(
        functools.partial(integrate_near_body, entries, radix),
        out_shape=(half(near), half(near)),
        in_specs=[pl.BlockSpec(memory_space=pltpu.SMEM), vmem, vmem],
        out_specs=(vmem, vmem),
        scratch_shapes=[total(near)],
        name="integrate_near",
        **options(1 / rows),
    )(table, lefts, weighted)
    return far_keep, far_send, near_keep, near_send


def index_of(row, col, s, count):
    return source_slot(row, source(col, s, count), count)


def product_body(count, *refs):
    lefts, rights, out = refs[:count], refs[count : 2 * count], refs[-2]
    stacked = refs[-1]
    for s in range(count):
        stacked[s] = rights[s][...]
    row, col = lax.axis_index("row"), lax.axis_index("col")
    found = None
    for s in range(count):
        term = jnp.dot(lefts[s][...], stacked[index_of(row, col, s, count)], preferred_element_type=jnp.float32)
        found = term if found is None else found + term
    out[...] = found.astype(out.dtype)


def product(lefts, rights, dtype):
    count = len(lefts)
    rows, columns = lefts[0].shape[0], rights[0].shape[1]
    vmem = pl.BlockSpec(memory_space=pltpu.VMEM)
    return pl.pallas_call(
        functools.partial(product_body, count),
        out_shape=jax.ShapeDtypeStruct((rows, columns), dtype),
        in_specs=[vmem] * (2 * count),
        out_specs=vmem,
        scratch_shapes=[pltpu.VMEM((count,) + rights[0].shape, rights[0].dtype)],
        cost_estimate=pl.CostEstimate(
            flops=2 * count * rows * columns * rights[0].shape[0],
            bytes_accessed=2 * count * (lefts[0].size + rights[0].size),
            transcendentals=0,
        ),
        compiler_params=pltpu.CompilerParams(vmem_limit_bytes=2 * VMEM_MARGIN),
        name="product",
    )(*lefts, *rights)


def gradient_body(pieces, count, *refs):
    number = len(pieces)
    own, other, rights = refs[:number], refs[number : 2 * number], refs[2 * number : 2 * number + count]
    out, stacked = refs[-2:]
    for s in range(count):
        stacked[s] = rights[s][...]
    blocks, size = own[0].shape[1], own[0].shape[2]
    row, col, side = lax.axis_index("row"), lax.axis_index("col"), lax.axis_index("panel")
    for which, parts in ((side, own), (1 - side, other)):
        found = None
        for slots, part in zip(pieces, parts):
            for k, s in enumerate(slots):
                left = jnp.concatenate([part[k, b] for b in range(blocks)], axis=1)
                term = jnp.dot(left, stacked[index_of(row, col, s, count)], preferred_element_type=jnp.float32)
                found = term if found is None else found + term
        out[pl.ds(which * size, size), :] = found


def program(
    basis_values,
    potential,
    pair_atoms,
    target_device,
    target_block,
    density,
    density_mask,
    inverse_intersection,
    inverse_mask,
):
    size = basis_values.shape[2]
    rows, cols, layers = lax.axis_size("row"), lax.axis_size("col"), lax.axis_size("panel")
    layer = lax.axis_index("panel")
    tile_blocks = density_mask.shape[0]
    per_owner = tile_blocks // layers * tile_blocks

    width = inverse_intersection.shape[1] // layers
    mask_width = inverse_mask.shape[1] // layers
    density_used = masked_blocks(density, density_mask, size)
    inverse_used = masked_blocks(
        lax.dynamic_slice_in_dim(inverse_intersection, layer * width, width, 1),
        lax.dynamic_slice_in_dim(inverse_mask, layer * mask_width, mask_width, 1),
        size,
    )
    lefts = [density_used] + [exchange(density_used, "col", s) for s in range(1, cols)]
    rights = [inverse_used] + [exchange(inverse_used, "row", s) for s in range(1, rows)]

    far_keep, far_send, near_keep, near_send = integrate(
        basis_values, potential, pair_atoms, target_device, target_block, (rows, cols, layers), per_owner
    )

    panel_tile = product(lefts, rights, jnp.bfloat16)
    panels = [panel_tile] + [exchange(panel_tile, "row", s) for s in range(1, rows)]

    def added(*terms):
        return sum(t.astype(jnp.float32) for t in terms[1:]) + terms[0].astype(jnp.float32)

    per_row = cols * per_owner
    far_got = exchange(far_send, "panel", 1)
    near_got = exchange(near_send, "panel", 1)
    parts = [added(near_keep, near_got).astype(jnp.bfloat16)] + [
        added(far_keep[s * per_row : (s + 1) * per_row], far_got[s * per_row : (s + 1) * per_row]).astype(jnp.bfloat16)
        for s in range(rows - 1)
    ]
    got = [exchange(parts[s], "row", s) for s in range(1, rows)]
    parts = [
        added(*[p[s * per_owner : (s + 1) * per_owner] for p in [parts[0]] + got]).astype(jnp.bfloat16)
        for s in range(cols)
    ]
    steps = [1 << k for k in range((cols - 1).bit_length())]
    live = dict(enumerate(parts))
    for step in steps[:-1]:
        kept = [s for s in live if not s & step]
        got = exchange(jnp.stack([live[s | step] for s in kept]), "col", step)
        live = {s: added(live[s], got[k]).astype(jnp.bfloat16) for k, s in enumerate(kept)}
    slots = list(live)
    got = exchange(jnp.stack([live[s] for s in slots]), "col", steps[-1])
    here = jnp.stack([added(live[s], got[slots.index(s ^ steps[-1])]).astype(jnp.bfloat16) for s in slots])
    pieces, own, other = [slots], [here], []
    for step in reversed(steps[:-1]):
        sent = own[0] if len(own) == 1 else jnp.concatenate(own)
        got = exchange(sent, "col", step)
        own.append(got)
        pieces.append([s | step for slots in pieces for s in slots])
    other = [exchange(piece, "panel", 1) for piece in own]
    vmem = pl.BlockSpec(memory_space=pltpu.VMEM)
    return pl.pallas_call(
        functools.partial(gradient_body, pieces, cols),
        out_shape=jax.ShapeDtypeStruct((layers * size, width), jnp.float32),
        in_specs=[vmem] * (len(own) + len(other) + rows),
        out_specs=vmem,
        scratch_shapes=[pltpu.VMEM((cols,) + panel_tile.shape, jnp.bfloat16)],
        compiler_params=pltpu.CompilerParams(vmem_limit_bytes=2 * VMEM_MARGIN),
        name="gradient",
    )(*own, *other, *panels)


def solution(mesh):
    placed = (
        P(("row", "col", "panel"), None, None),
        P(("row", "col", "panel")),
        P(None, ("row", "col", "panel")),
        P(("row", "col", "panel"), None),
        P(("row", "col", "panel")),
        P("row", "col"),
        P("row", "col"),
        P("row", "col"),
        P("row", "col"),
    )
    return jax.shard_map(program, mesh=mesh, in_specs=placed, out_specs=P("row", ("col", "panel")), check_vma=False)
```

```python
import functools

import jax
import jax.numpy as jnp
from jax import lax
from jax.experimental import pallas as pl
from jax.experimental.pallas import tpu as pltpu
from jax.sharding import PartitionSpec as P


UNROLL = 16
REST = 4
IN_FLIGHT = 6
VMEM_LIMIT = 36 * 1024 * 1024
VMEM_MARGIN = 4 * 1024 * 1024


def target(i, s, n):
    return i ^ s if n & (n - 1) == 0 else (i + s) % n


def source(i, s, n):
    return i ^ s if n & (n - 1) == 0 else (i - s) % n


def target_slot(i, j, n):
    return i ^ j if n & (n - 1) == 0 else (j - i) % n


def source_slot(i, j, n):
    return i ^ j if n & (n - 1) == 0 else (i - j) % n


def exchange(value, axis, slot):
    n = lax.axis_size(axis)
    return lax.ppermute(value, axis, [(i, target(i, slot, n)) for i in range(n)])


def masked_blocks(matrix, block_mask, block_size):
    mask_rows, mask_cols = block_mask.shape
    shaped = matrix.reshape(mask_rows, block_size, mask_cols, block_size)
    factor = block_mask.astype(matrix.dtype)[:, None, :, None]
    return (shaped * factor).reshape(mask_rows * block_size, mask_cols * block_size)


def place_of(sizes, per_owner, owner, block):
    rows, cols, layers = sizes
    far_layer = target_slot(lax.axis_index("panel"), owner % layers, layers)
    far_col = target_slot(lax.axis_index("col"), (owner // layers) % cols, cols)
    far_row = target_slot(lax.axis_index("row"), owner // (layers * cols), rows)
    near = (far_row == 0).astype(jnp.int32)
    at = jnp.where(near == 1, far_layer, far_layer * (rows - 1) + far_row - 1)
    return near, (at * cols + far_col) * per_owner + block + 1


def across(row):
    return jnp.broadcast_to(row, (row.shape[1], row.shape[1])).T


def most_units(parts, atoms):
    return (parts + atoms) // 2 + UNROLL


def plan(sizes, per_owner, atoms, radix, pairs, owner, block):
    parts = owner.shape[1]
    left, right = pairs[0:1, :], pairs[1:2, :]
    near, slot = place_of(sizes, per_owner, owner, block)
    key = left + near * atoms
    lane = lax.broadcasted_iota(jnp.int32, (parts, parts), 1)
    sublane = lax.broadcasted_iota(jnp.int32, (parts, parts), 0)
    earlier = (across(key) == key) & (sublane < lane)
    rank = jnp.sum(earlier.astype(jnp.int32), axis=0, keepdims=True)
    which = lax.broadcasted_iota(jnp.int32, (2 * atoms, parts), 0)
    members = jnp.sum((which == key).astype(jnp.int32), axis=1, keepdims=True)
    units = (members + 1) // 2
    before = (which < key) & ((which >= atoms) == (near == 1))
    start = jnp.sum(jnp.where(before, units, 0), axis=0, keepdims=True)
    entries = 2 * most_units(parts, atoms)
    at = 2 * start + rank + near * entries
    width = -(-(2 * entries + 2) // parts) * parts
    code = (left * radix + right) * radix + slot
    place = lax.broadcasted_iota(jnp.int32, (parts, width), 1)
    here = jnp.concatenate([across(at)] * (width // parts), axis=1) == place
    table = jnp.sum(jnp.where(here, jnp.concatenate([across(code)] * (width // parts), axis=1), 0), axis=0, keepdims=True)
    far_units = jnp.sum(jnp.where(which[:, 0:1] < atoms, units, 0), axis=0, keepdims=True)
    near_units = jnp.sum(jnp.where(which[:, 0:1] < atoms, 0, units), axis=0, keepdims=True)
    place = place[0:1, :]
    return jnp.where(place == width - 2, far_units, jnp.where(place == width - 1, near_units, table))


def accumulate(chunk, entries, radix, table, lefts, weighted, total):
    size = lefts.shape[1]

    def units(first, number):
        for j in range(number):
            at = chunk * entries + 2 * (first + j)
            one, two = table[0, at], table[0, at + 1]
            rights = jnp.concatenate(
                [weighted[(one // radix) % radix], weighted[(two // radix) % radix]], axis=1
            )
            found = jnp.dot(lefts[one // (radix * radix)], rights, preferred_element_type=jnp.float32)
            total[one % radix] += found[:, :size]
            total[two % radix] += found[:, size:]

    def many(i, carry):
        units(i * UNROLL, UNROLL)
        return carry

    def few(i, carry):
        units(whole * UNROLL + i * REST, REST)
        return carry

    count = table[0, table.shape[1] - 2 + chunk]
    whole = count // UNROLL
    lax.fori_loop(0, whole, many, 0)
    lax.fori_loop(0, (count - whole * UNROLL + REST - 1) // REST, few, 0)


def clear(total):
    def zero(i, carry):
        total[i] = jnp.zeros(total.shape[1:], jnp.float32)
        return carry

    lax.fori_loop(0, total.shape[0], zero, 0)


def put(total, keep_refs, send_refs):
    share = send_refs[0].shape[0]
    half = share * len(send_refs)

    def one(i, carry):
        for k, (keep_ref, send_ref) in enumerate(zip(keep_refs, send_refs)):
            keep_ref[i] = total[k * share + i + 1].astype(jnp.bfloat16)
            send_ref[i] = total[half + k * share + i + 1].astype(jnp.bfloat16)
        return carry

    lax.fori_loop(0, share, one, 0)


def integrate_far_body(
    sizes, per_owner, entries, radix, pair_ref, owner_ref, block_ref, basis_ref, pot_ref,
    lefts, weighted, table_ref, *refs,
):
    far_rows = sizes[0] - 1
    keep_refs, send_refs = refs[:far_rows], refs[far_rows : 2 * far_rows]
    pairs, owner, block, pot, basis, pot_cols, total, table, small_sems, arrived = refs[2 * far_rows :]
    atoms, points, size = basis.shape
    small = [
        pltpu.make_async_copy(source_ref, to, small_sems.at[k])
        for k, (source_ref, to) in enumerate(
            ((pair_ref, pairs), (owner_ref, owner), (block_ref, block), (pot_ref, pot))
        )
    ]
    for copy in small:
        copy.start()

    def fetch(a):
        return pltpu.make_async_copy(basis_ref.at[a], basis.at[a], arrived.at[a])

    for a in range(IN_FLIGHT):
        fetch(a).start()
    clear(total)
    for copy in small:
        copy.wait()
    table_ref[...] = plan(sizes, per_owner, atoms, radix, pairs[...], owner[...], block[...])
    to_scalar = pltpu.make_async_copy(table_ref, table, small_sems.at[4])
    to_scalar.start()
    for k in range(points // size):
        pot_cols[k * size : (k + 1) * size, :] = across(pot[k : k + 1, :])

    def weigh(a, carry):
        fetch(a).wait()

        @pl.when(a + IN_FLIGHT < atoms)
        def _():
            fetch(a + IN_FLIGHT).start()

        for k in range(points // size):
            at = slice(k * size, (k + 1) * size)
            values = basis[a, at, :]
            weighted[a, at, :] = (values.astype(jnp.float32) * pot_cols[at, :]).astype(jnp.bfloat16)
            lefts[a, :, at] = values.T
        return carry

    lax.fori_loop(0, atoms, weigh, 0)
    to_scalar.wait()
    accumulate(0, entries, radix, table, lefts, weighted, total)
    put(total, keep_refs, send_refs)


def integrate_near_body(entries, radix, table, lefts, weighted, keep_ref, send_ref, total):
    clear(total)
    accumulate(1, entries, radix, table, lefts, weighted, total)
    put(total, [keep_ref], [send_ref])


def integrate(basis_values, potential, pair_atoms, target_device, target_block, sizes, per_owner):
    atoms, points, size = basis_values.shape
    parts = target_block.shape[0]
    rows, cols, layers = sizes
    per_row = cols * per_owner
    far, near = layers * (rows - 1) * per_row, layers * per_row
    entries = 2 * most_units(parts, atoms)
    width = -(-(2 * entries + 2) // parts) * parts
    radix = pl.next_power_of_2(max(far + 1, near + 1, atoms))
    vmem = pl.BlockSpec(memory_space=pltpu.VMEM)
    hbm = pl.BlockSpec(memory_space=pltpu.HBM)

    def half(blocks):
        return jax.ShapeDtypeStruct((blocks // 2, size, size), jnp.bfloat16)

    def total(blocks):
        return pltpu.VMEM((blocks + 1, size, size), jnp.float32)

    def options(share):
        return dict(
            compiler_params=pltpu.CompilerParams(vmem_limit_bytes=VMEM_LIMIT),
            cost_estimate=pl.CostEstimate(
                flops=int(4 * parts * points * size * size * share),
                bytes_accessed=4 * basis_values.size,
                transcendentals=0,
            ),
        )

    def in_hbm(array):
        return pltpu.with_memory_space_constraint(array, pltpu.HBM)

    lefts, weighted, table, *found = pl.pallas_call(
        functools.partial(integrate_far_body, sizes, per_owner, entries, radix),
        out_shape=(
            jax.ShapeDtypeStruct((atoms, size, points), jnp.bfloat16),
            jax.ShapeDtypeStruct((atoms, points, size), jnp.bfloat16),
            jax.ShapeDtypeStruct((1, width), jnp.int32),
            *[half(near)] * (2 * (rows - 1)),
        ),
        in_specs=[hbm] * 5,
        out_specs=(vmem,) * (2 * rows + 1),
        scratch_shapes=[
            pltpu.VMEM((2, parts), jnp.int32),
            pltpu.VMEM((1, parts), jnp.int32),
            pltpu.VMEM((1, parts), jnp.int32),
            pltpu.VMEM((points // size, size), jnp.float32),
            pltpu.VMEM((atoms, points, size), jnp.bfloat16),
            pltpu.VMEM((points, size), jnp.float32),
            total(far),
            pltpu.SMEM((1, width), jnp.int32),
            pltpu.SemaphoreType.DMA((5,)),
            pltpu.SemaphoreType.DMA((atoms,)),
        ],
        name="integrate_far",
        **options(1 - 1 / rows),
    )(
        in_hbm(pair_atoms),
        in_hbm(target_device.reshape(1, parts)),
        in_hbm(target_block.reshape(1, parts)),
        in_hbm(basis_values),
        in_hbm(potential.reshape(points // size, size)),
    )
    near_keep, near_send = pl.pallas_call(
        functools.partial(integrate_near_body, entries, radix),
        out_shape=(half(near), half(near)),
        in_specs=[pl.BlockSpec(memory_space=pltpu.SMEM), vmem, vmem],
        out_specs=(vmem, vmem),
        scratch_shapes=[total(near)],
        name="integrate_near",
        **options(1 / rows),
    )(table, lefts, weighted)
    return found[: rows - 1], found[rows - 1 :], near_keep, near_send


def index_of(row, col, s, count):
    return source_slot(row, source(col, s, count), count)


def product_body(count, *refs):
    lefts, rights, out = refs[:count], refs[count : 2 * count], refs[-2]
    stacked = refs[-1]
    for s in range(count):
        stacked[s] = rights[s][...]
    row, col = lax.axis_index("row"), lax.axis_index("col")
    found = None
    for s in range(count):
        term = jnp.dot(lefts[s][...], stacked[index_of(row, col, s, count)], preferred_element_type=jnp.float32)
        found = term if found is None else found + term
    out[...] = found.astype(out.dtype)


def product(lefts, rights, dtype):
    count = len(lefts)
    rows, columns = lefts[0].shape[0], rights[0].shape[1]
    vmem = pl.BlockSpec(memory_space=pltpu.VMEM)
    return pl.pallas_call(
        functools.partial(product_body, count),
        out_shape=jax.ShapeDtypeStruct((rows, columns), dtype),
        in_specs=[vmem] * (2 * count),
        out_specs=vmem,
        scratch_shapes=[pltpu.VMEM((count,) + rights[0].shape, rights[0].dtype)],
        cost_estimate=pl.CostEstimate(
            flops=2 * count * rows * columns * rights[0].shape[0],
            bytes_accessed=2 * count * (lefts[0].size + rights[0].size),
            transcendentals=0,
        ),
        compiler_params=pltpu.CompilerParams(vmem_limit_bytes=2 * VMEM_MARGIN),
        name="product",
    )(*lefts, *rights)


def gradient_body(pieces, count, *refs):
    number = len(pieces)
    own, other, rights = refs[:number], refs[number : 2 * number], refs[2 * number : 2 * number + count]
    out, stacked = refs[-2:]
    for s in range(count):
        stacked[s] = rights[s][...]
    blocks, size = own[0].shape[1], own[0].shape[2]
    row, col, side = lax.axis_index("row"), lax.axis_index("col"), lax.axis_index("panel")
    for which, parts in ((side, own), (1 - side, other)):
        found = None
        for slots, part in zip(pieces, parts):
            for k, s in enumerate(slots):
                left = jnp.concatenate([part[k, b] for b in range(blocks)], axis=1)
                term = jnp.dot(left, stacked[index_of(row, col, s, count)], preferred_element_type=jnp.float32)
                found = term if found is None else found + term
        out[pl.ds(which * size, size), :] = found


def program(
    basis_values,
    potential,
    pair_atoms,
    target_device,
    target_block,
    density,
    density_mask,
    inverse_intersection,
    inverse_mask,
):
    size = basis_values.shape[2]
    rows, cols, layers = lax.axis_size("row"), lax.axis_size("col"), lax.axis_size("panel")
    layer = lax.axis_index("panel")
    tile_blocks = density_mask.shape[0]
    per_owner = tile_blocks // layers * tile_blocks

    width = inverse_intersection.shape[1] // layers
    mask_width = inverse_mask.shape[1] // layers
    density_used = masked_blocks(density, density_mask, size)
    inverse_used = masked_blocks(
        lax.dynamic_slice_in_dim(inverse_intersection, layer * width, width, 1),
        lax.dynamic_slice_in_dim(inverse_mask, layer * mask_width, mask_width, 1),
        size,
    )
    lefts = [density_used] + [exchange(density_used, "col", s) for s in range(1, cols)]
    rights = [inverse_used] + [exchange(inverse_used, "row", s) for s in range(1, rows)]

    far_keep, far_send, near_keep, near_send = integrate(
        basis_values, potential, pair_atoms, target_device, target_block, (rows, cols, layers), per_owner
    )

    panel_tile = product(lefts, rights, jnp.bfloat16)
    panels = [panel_tile] + [exchange(panel_tile, "row", s) for s in range(1, rows)]

    def added(*terms):
        return sum(t.astype(jnp.float32) for t in terms[1:]) + terms[0].astype(jnp.float32)

    far_got = [exchange(far_send[s - 1], "panel", 1) for s in range(1, rows)]
    near_got = exchange(near_send, "panel", 1)
    parts = [added(near_keep, near_got).astype(jnp.bfloat16)] + [
        added(far_keep[s], far_got[s]).astype(jnp.bfloat16)
        for s in range(rows - 1)
    ]
    got = [exchange(parts[s], "row", s) for s in range(1, rows)]
    parts = [
        added(*[p[s * per_owner : (s + 1) * per_owner] for p in [parts[0]] + got]).astype(jnp.bfloat16)
        for s in range(cols)
    ]
    steps = [1 << k for k in range((cols - 1).bit_length())]
    live = dict(enumerate(parts))
    for step in steps[:-1]:
        kept = [s for s in live if not s & step]
        got = exchange(jnp.stack([live[s | step] for s in kept]), "col", step)
        live = {s: added(live[s], got[k]).astype(jnp.bfloat16) for k, s in enumerate(kept)}
    slots = list(live)
    got = exchange(jnp.stack([live[s] for s in slots]), "col", steps[-1])
    here = jnp.stack([added(live[s], got[slots.index(s ^ steps[-1])]).astype(jnp.bfloat16) for s in slots])
    pieces, own, other = [slots], [here], []
    for step in reversed(steps[:-1]):
        sent = own[0] if len(own) == 1 else jnp.concatenate(own)
        got = exchange(sent, "col", step)
        own.append(got)
        pieces.append([s | step for slots in pieces for s in slots])
    other = [exchange(piece, "panel", 1) for piece in own]
    vmem = pl.BlockSpec(memory_space=pltpu.VMEM)
    return pl.pallas_call(
        functools.partial(gradient_body, pieces, cols),
        out_shape=jax.ShapeDtypeStruct((layers * size, width), jnp.float32),
        in_specs=[vmem] * (len(own) + len(other) + rows),
        out_specs=vmem,
        scratch_shapes=[pltpu.VMEM((cols,) + panel_tile.shape, jnp.bfloat16)],
        compiler_params=pltpu.CompilerParams(vmem_limit_bytes=2 * VMEM_MARGIN),
        name="gradient",
    )(*own, *other, *panels)


def solution(mesh):
    placed = (
        P(("row", "col", "panel"), None, None),
        P(("row", "col", "panel")),
        P(None, ("row", "col", "panel")),
        P(("row", "col", "panel"), None),
        P(("row", "col", "panel")),
        P("row", "col"),
        P("row", "col"),
        P("row", "col"),
        P("row", "col"),
    )
    return jax.shard_map(program, mesh=mesh, in_specs=placed, out_specs=P("row", ("col", "panel")), check_vma=False)
```

```python
import functools

import jax
import jax.numpy as jnp
from jax import lax
from jax.experimental import pallas as pl
from jax.experimental.pallas import tpu as pltpu
from jax.sharding import PartitionSpec as P


UNROLLS = 24, 16
REST = 4
IN_FLIGHT = 6
VMEM_LIMIT = 36 * 1024 * 1024
VMEM_MARGIN = 4 * 1024 * 1024


def target(i, s, n):
    return i ^ s if n & (n - 1) == 0 else (i + s) % n


def source(i, s, n):
    return i ^ s if n & (n - 1) == 0 else (i - s) % n


def target_slot(i, j, n):
    return i ^ j if n & (n - 1) == 0 else (j - i) % n


def source_slot(i, j, n):
    return i ^ j if n & (n - 1) == 0 else (i - j) % n


def exchange(value, axis, slot):
    n = lax.axis_size(axis)
    return lax.ppermute(value, axis, [(i, target(i, slot, n)) for i in range(n)])


def masked_blocks(matrix, block_mask, block_size):
    mask_rows, mask_cols = block_mask.shape
    shaped = matrix.reshape(mask_rows, block_size, mask_cols, block_size)
    factor = block_mask.astype(matrix.dtype)[:, None, :, None]
    return (shaped * factor).reshape(mask_rows * block_size, mask_cols * block_size)


def place_of(sizes, per_owner, owner, block):
    rows, cols, layers = sizes
    far_layer = target_slot(lax.axis_index("panel"), owner % layers, layers)
    far_col = target_slot(lax.axis_index("col"), (owner // layers) % cols, cols)
    far_row = target_slot(lax.axis_index("row"), owner // (layers * cols), rows)
    near = (far_row == 0).astype(jnp.int32)
    at = jnp.where(near == 1, far_layer, far_layer * (rows - 1) + far_row - 1)
    return near, (at * cols + far_col) * per_owner + block + 1


def across(row):
    return jnp.broadcast_to(row, (row.shape[1], row.shape[1])).T


def most_units(parts, atoms):
    return (parts + atoms) // 2 + REST


def plan(sizes, per_owner, atoms, radix, pairs, owner, block):
    parts = owner.shape[1]
    left, right = pairs[0:1, :], pairs[1:2, :]
    near, slot = place_of(sizes, per_owner, owner, block)
    key = left + near * atoms
    lane = lax.broadcasted_iota(jnp.int32, (parts, parts), 1)
    sublane = lax.broadcasted_iota(jnp.int32, (parts, parts), 0)
    earlier = (across(key) == key) & (sublane < lane)
    rank = jnp.sum(earlier.astype(jnp.int32), axis=0, keepdims=True)
    which = lax.broadcasted_iota(jnp.int32, (2 * atoms, parts), 0)
    members = jnp.sum((which == key).astype(jnp.int32), axis=1, keepdims=True)
    units = (members + 1) // 2
    before = (which < key) & ((which >= atoms) == (near == 1))
    start = jnp.sum(jnp.where(before, units, 0), axis=0, keepdims=True)
    entries = 2 * most_units(parts, atoms)
    at = 2 * start + rank + near * entries
    width = -(-(2 * entries + 2) // parts) * parts
    code = (left * radix + right) * radix + slot
    place = lax.broadcasted_iota(jnp.int32, (parts, width), 1)
    here = jnp.concatenate([across(at)] * (width // parts), axis=1) == place
    table = jnp.sum(jnp.where(here, jnp.concatenate([across(code)] * (width // parts), axis=1), 0), axis=0, keepdims=True)
    far_units = jnp.sum(jnp.where(which[:, 0:1] < atoms, units, 0), axis=0, keepdims=True)
    near_units = jnp.sum(jnp.where(which[:, 0:1] < atoms, 0, units), axis=0, keepdims=True)
    place = place[0:1, :]
    return jnp.where(place == width - 2, far_units, jnp.where(place == width - 1, near_units, table))


def accumulate(chunk, entries, radix, table, lefts, weighted, total):
    size, unroll = lefts.shape[1], UNROLLS[chunk]

    def units(first, number):
        for j in range(number):
            at = chunk * entries + 2 * (first + j)
            one, two = table[0, at], table[0, at + 1]
            rights = jnp.concatenate(
                [weighted[(one // radix) % radix], weighted[(two // radix) % radix]], axis=1
            )
            found = jnp.dot(lefts[one // (radix * radix)], rights, preferred_element_type=jnp.float32)
            total[one % radix] += found[:, :size]
            total[two % radix] += found[:, size:]

    def many(i, carry):
        units(i * unroll, unroll)
        return carry

    def few(i, carry):
        units(whole * unroll + i * REST, REST)
        return carry

    count = table[0, table.shape[1] - 2 + chunk]
    whole = count // unroll
    lax.fori_loop(0, whole, many, 0)
    lax.fori_loop(0, (count - whole * unroll + REST - 1) // REST, few, 0)


def clear(total):
    def zero(i, carry):
        total[i] = jnp.zeros(total.shape[1:], jnp.float32)
        return carry

    lax.fori_loop(0, total.shape[0], zero, 0)


def put(total, keep_refs, send_refs):
    share = send_refs[0].shape[0]
    half = share * len(send_refs)

    def one(i, carry):
        for k, (keep_ref, send_ref) in enumerate(zip(keep_refs, send_refs)):
            keep_ref[i] = total[k * share + i + 1].astype(jnp.bfloat16)
            send_ref[i] = total[half + k * share + i + 1].astype(jnp.bfloat16)
        return carry

    lax.fori_loop(0, share, one, 0)


def integrate_far_body(
    sizes, per_owner, entries, radix, pair_ref, owner_ref, block_ref, basis_ref, pot_ref,
    lefts, weighted, table_ref, *refs,
):
    far_rows = sizes[0] - 1
    keep_refs, send_refs = refs[:far_rows], refs[far_rows : 2 * far_rows]
    pairs, owner, block, pot, basis, pot_cols, total, table, small_sems, arrived = refs[2 * far_rows :]
    atoms, points, size = basis.shape
    small = [
        pltpu.make_async_copy(source_ref, to, small_sems.at[k])
        for k, (source_ref, to) in enumerate(
            ((pair_ref, pairs), (owner_ref, owner), (block_ref, block), (pot_ref, pot))
        )
    ]
    for copy in small:
        copy.start()

    def fetch(a):
        return pltpu.make_async_copy(basis_ref.at[a], basis.at[a], arrived.at[a])

    for a in range(IN_FLIGHT):
        fetch(a).start()
    clear(total)
    for copy in small:
        copy.wait()
    table_ref[...] = plan(sizes, per_owner, atoms, radix, pairs[...], owner[...], block[...])
    to_scalar = pltpu.make_async_copy(table_ref, table, small_sems.at[4])
    to_scalar.start()
    for k in range(points // size):
        pot_cols[k * size : (k + 1) * size, :] = across(pot[k : k + 1, :])

    def weigh(a, carry):
        fetch(a).wait()

        @pl.when(a + IN_FLIGHT < atoms)
        def _():
            fetch(a + IN_FLIGHT).start()

        for k in range(points // size):
            at = slice(k * size, (k + 1) * size)
            values = basis[a, at, :]
            weighted[a, at, :] = (values.astype(jnp.float32) * pot_cols[at, :]).astype(jnp.bfloat16)
            lefts[a, :, at] = values.T
        return carry

    lax.fori_loop(0, atoms, weigh, 0)
    to_scalar.wait()
    accumulate(0, entries, radix, table, lefts, weighted, total)
    put(total, keep_refs, send_refs)


def integrate_near_body(entries, radix, table, lefts, weighted, keep_ref, send_ref, total):
    clear(total)
    accumulate(1, entries, radix, table, lefts, weighted, total)
    put(total, [keep_ref], [send_ref])


def integrate(basis_values, potential, pair_atoms, target_device, target_block, sizes, per_owner):
    atoms, points, size = basis_values.shape
    parts = target_block.shape[0]
    rows, cols, layers = sizes
    per_row = cols * per_owner
    far, near = layers * (rows - 1) * per_row, layers * per_row
    entries = 2 * most_units(parts, atoms)
    width = -(-(2 * entries + 2) // parts) * parts
    radix = pl.next_power_of_2(max(far + 1, near + 1, atoms))
    vmem = pl.BlockSpec(memory_space=pltpu.VMEM)
    hbm = pl.BlockSpec(memory_space=pltpu.HBM)

    def half(blocks):
        return jax.ShapeDtypeStruct((blocks // 2, size, size), jnp.bfloat16)

    def total(blocks):
        return pltpu.VMEM((blocks + 1, size, size), jnp.float32)

    def options(share):
        return dict(
            compiler_params=pltpu.CompilerParams(vmem_limit_bytes=VMEM_LIMIT),
            cost_estimate=pl.CostEstimate(
                flops=int(4 * parts * points * size * size * share),
                bytes_accessed=4 * basis_values.size,
                transcendentals=0,
            ),
        )

    def in_hbm(array):
        return pltpu.with_memory_space_constraint(array, pltpu.HBM)

    lefts, weighted, table, *found = pl.pallas_call(
        functools.partial(integrate_far_body, sizes, per_owner, entries, radix),
        out_shape=(
            jax.ShapeDtypeStruct((atoms, size, points), jnp.bfloat16),
            jax.ShapeDtypeStruct((atoms, points, size), jnp.bfloat16),
            jax.ShapeDtypeStruct((1, width), jnp.int32),
            *[half(near)] * (2 * (rows - 1)),
        ),
        in_specs=[hbm] * 5,
        out_specs=(vmem,) * (2 * rows + 1),
        scratch_shapes=[
            pltpu.VMEM((2, parts), jnp.int32),
            pltpu.VMEM((1, parts), jnp.int32),
            pltpu.VMEM((1, parts), jnp.int32),
            pltpu.VMEM((points // size, size), jnp.float32),
            pltpu.VMEM((atoms, points, size), jnp.bfloat16),
            pltpu.VMEM((points, size), jnp.float32),
            total(far),
            pltpu.SMEM((1, width), jnp.int32),
            pltpu.SemaphoreType.DMA((5,)),
            pltpu.SemaphoreType.DMA((atoms,)),
        ],
        name="integrate_far",
        **options(1 - 1 / rows),
    )(
        in_hbm(pair_atoms),
        in_hbm(target_device.reshape(1, parts)),
        in_hbm(target_block.reshape(1, parts)),
        in_hbm(basis_values),
        in_hbm(potential.reshape(points // size, size)),
    )
    near_keep, near_send = pl.pallas_call(
        functools.partial(integrate_near_body, entries, radix),
        out_shape=(half(near), half(near)),
        in_specs=[pl.BlockSpec(memory_space=pltpu.SMEM), vmem, vmem],
        out_specs=(vmem, vmem),
        scratch_shapes=[total(near)],
        name="integrate_near",
        **options(1 / rows),
    )(table, lefts, weighted)
    return found[: rows - 1], found[rows - 1 :], near_keep, near_send


def index_of(row, col, s, count):
    return source_slot(row, source(col, s, count), count)


def product_body(count, *refs):
    lefts, rights, out = refs[:count], refs[count : 2 * count], refs[-2]
    stacked = refs[-1]
    for s in range(count):
        stacked[s] = rights[s][...]
    row, col = lax.axis_index("row"), lax.axis_index("col")
    found = None
    for s in range(count):
        term = jnp.dot(lefts[s][...], stacked[index_of(row, col, s, count)], preferred_element_type=jnp.float32)
        found = term if found is None else found + term
    out[...] = found.astype(out.dtype)


def product(lefts, rights, dtype):
    count = len(lefts)
    rows, columns = lefts[0].shape[0], rights[0].shape[1]
    vmem = pl.BlockSpec(memory_space=pltpu.VMEM)
    return pl.pallas_call(
        functools.partial(product_body, count),
        out_shape=jax.ShapeDtypeStruct((rows, columns), dtype),
        in_specs=[vmem] * (2 * count),
        out_specs=vmem,
        scratch_shapes=[pltpu.VMEM((count,) + rights[0].shape, rights[0].dtype)],
        cost_estimate=pl.CostEstimate(
            flops=2 * count * rows * columns * rights[0].shape[0],
            bytes_accessed=2 * count * (lefts[0].size + rights[0].size),
            transcendentals=0,
        ),
        compiler_params=pltpu.CompilerParams(vmem_limit_bytes=2 * VMEM_MARGIN),
        name="product",
    )(*lefts, *rights)


def gradient_body(pieces, count, *refs):
    number = len(pieces)
    own, other, rights = refs[:number], refs[number : 2 * number], refs[2 * number : 2 * number + count]
    out, stacked = refs[-2:]
    for s in range(count):
        stacked[s] = rights[s][...]
    blocks, size = own[0].shape[1], own[0].shape[2]
    row, col, side = lax.axis_index("row"), lax.axis_index("col"), lax.axis_index("panel")
    for which, parts in ((side, own), (1 - side, other)):
        found = None
        for slots, part in zip(pieces, parts):
            for k, s in enumerate(slots):
                left = jnp.concatenate([part[k, b] for b in range(blocks)], axis=1)
                term = jnp.dot(left, stacked[index_of(row, col, s, count)], preferred_element_type=jnp.float32)
                found = term if found is None else found + term
        out[pl.ds(which * size, size), :] = found


def program(
    basis_values,
    potential,
    pair_atoms,
    target_device,
    target_block,
    density,
    density_mask,
    inverse_intersection,
    inverse_mask,
):
    size = basis_values.shape[2]
    rows, cols, layers = lax.axis_size("row"), lax.axis_size("col"), lax.axis_size("panel")
    layer = lax.axis_index("panel")
    tile_blocks = density_mask.shape[0]
    per_owner = tile_blocks // layers * tile_blocks

    width = inverse_intersection.shape[1] // layers
    mask_width = inverse_mask.shape[1] // layers
    density_used = masked_blocks(density, density_mask, size)
    inverse_used = masked_blocks(
        lax.dynamic_slice_in_dim(inverse_intersection, layer * width, width, 1),
        lax.dynamic_slice_in_dim(inverse_mask, layer * mask_width, mask_width, 1),
        size,
    )
    lefts = [density_used] + [exchange(density_used, "col", s) for s in range(1, cols)]
    rights = [inverse_used] + [exchange(inverse_used, "row", s) for s in range(1, rows)]

    far_keep, far_send, near_keep, near_send = integrate(
        basis_values, potential, pair_atoms, target_device, target_block, (rows, cols, layers), per_owner
    )

    panel_tile = product(lefts, rights, jnp.bfloat16)
    panels = [panel_tile] + [exchange(panel_tile, "row", s) for s in range(1, rows)]

    def added(*terms):
        return sum(t.astype(jnp.float32) for t in terms[1:]) + terms[0].astype(jnp.float32)

    far_got = [exchange(far_send[s - 1], "panel", 1) for s in range(1, rows)]
    near_got = exchange(near_send, "panel", 1)
    parts = [added(near_keep, near_got).astype(jnp.bfloat16)] + [
        added(far_keep[s], far_got[s]).astype(jnp.bfloat16)
        for s in range(rows - 1)
    ]
    got = [exchange(parts[s], "row", s) for s in range(1, rows)]
    parts = [
        added(*[p[s * per_owner : (s + 1) * per_owner] for p in [parts[0]] + got]).astype(jnp.bfloat16)
        for s in range(cols)
    ]
    steps = [1 << k for k in range((cols - 1).bit_length())]
    live = dict(enumerate(parts))
    for step in steps[:-1]:
        kept = [s for s in live if not s & step]
        got = exchange(jnp.stack([live[s | step] for s in kept]), "col", step)
        live = {s: added(live[s], got[k]).astype(jnp.bfloat16) for k, s in enumerate(kept)}
    slots = list(live)
    got = exchange(jnp.stack([live[s] for s in slots]), "col", steps[-1])
    here = jnp.stack([added(live[s], got[slots.index(s ^ steps[-1])]).astype(jnp.bfloat16) for s in slots])
    pieces, own, other = [slots], [here], []
    for step in reversed(steps[:-1]):
        sent = own[0] if len(own) == 1 else jnp.concatenate(own)
        got = exchange(sent, "col", step)
        own.append(got)
        pieces.append([s | step for slots in pieces for s in slots])
    other = [exchange(piece, "panel", 1) for piece in own]
    vmem = pl.BlockSpec(memory_space=pltpu.VMEM)
    return pl.pallas_call(
        functools.partial(gradient_body, pieces, cols),
        out_shape=jax.ShapeDtypeStruct((layers * size, width), jnp.float32),
        in_specs=[vmem] * (len(own) + len(other) + rows),
        out_specs=vmem,
        scratch_shapes=[pltpu.VMEM((cols,) + panel_tile.shape, jnp.bfloat16)],
        compiler_params=pltpu.CompilerParams(vmem_limit_bytes=2 * VMEM_MARGIN),
        name="gradient",
    )(*own, *other, *panels)


def solution(mesh):
    placed = (
        P(("row", "col", "panel"), None, None),
        P(("row", "col", "panel")),
        P(None, ("row", "col", "panel")),
        P(("row", "col", "panel"), None),
        P(("row", "col", "panel")),
        P("row", "col"),
        P("row", "col"),
        P("row", "col"),
        P("row", "col"),
    )
    return jax.shard_map(program, mesh=mesh, in_specs=placed, out_specs=P("row", ("col", "panel")), check_vma=False)
```
